32 devices in a mesh: groups: 2 (over y), blk: 4 (over z), tile: 2 (over x), pair: 2 (over core).
Axes of the slice: x: 2, y: 2, z: 4, core: 2. Of those that a mesh axis runs over, the one named last changes fastest.
Arguments:
- left_tokens: bfloat16 [4, 1536, 768], P(('groups', 'pair'), 'blk', 'tile'), parts along dimension 0, may hold values from -32 to 32
- right_tokens: bfloat16 [4, 1536, 768], P(('groups', 'pair'), 'blk', 'tile'), parts along dimension 0, may hold values from -32 to 32
- self_qkv: bfloat16 [3, 768, 512], P(None, None, 'tile'), may hold values from -1 to 1
- self_out: bfloat16 [512, 768], P('tile'), may hold values from -0.25 to 0.25
- cross_qkv: bfloat16 [3, 768, 512], P(None, None, 'tile'), may hold values from -1 to 1
- cross_out: bfloat16 [512, 768], P('tile'), may hold values from -0.25 to 0.25
- reassemble: bfloat16 [768, 256], P('tile'), may hold values from -0.21875 to 0.21875
- conv_weight: bfloat16 [3, 3, 256, 256], replicated, may hold values from -0.125 to 0.125
Outputs:
- joined: bfloat16 [4, 12, 128, 256], P(('groups', 'pair'), 'blk', 'tile'), parts along dimension 0
The draws below stay inside these ranges and needn't reach their ends.
There are 2 independent parts, one for each index of `groups`. The reference program is written for one: setup_inputs(seed, part) draws one part's arguments, and reference() takes and returns one part's arrays. A program takes and returns all parts, laid end to end along the dimension named above; an argument that names none is the same for every part. Nothing has to cross between parts.
All inputs are finite; a program needn't handle non-finite values.
Results may differ from the reference program's by a relative error of at most 0.018.
Values may be sent and summed in bfloat16 or wider, within the bound.
A program may use at most 64 MiB of HBM per device.

```python
import math
import jax
import jax.numpy as jnp
from jax import lax

D = 768
HEADS = 8
HD = 64
CH = 256
GRID_W = 128
PAIRS = 2
GRID_H = 12
LEN = 1536


def token_field(key):
    keys = jax.random.split(key, 3)
    noise = jax.random.truncated_normal(keys[0], -4.0, 4.0, (PAIRS, LEN, D), jnp.float32)
    row_scale = jnp.exp(jax.random.uniform(keys[1], (PAIRS, LEN, 1), jnp.float32, math.log(0.3), math.log(3.0)))
    column_scale = jnp.exp(jax.random.uniform(keys[2], (D,), jnp.float32, math.log(0.2), math.log(2.0)))
    field = noise * column_scale
    return (field * row_scale).astype(jnp.bfloat16)


def projection_weights(key):
    keys = jax.random.split(key, 1)
    columns = HEADS * HD
    scales = jnp.array([1.67, 1.67, 1.0], jnp.float32)[:, None, None] / math.sqrt(D)
    weights = jax.random.truncated_normal(keys[0], -4.0, 4.0, (3, D, columns), jnp.float32) * scales
    return weights.astype(jnp.bfloat16)


def draw_left_tokens(key, part):
    return token_field(jax.random.fold_in(key, 3))


def draw_right_tokens(key, part):
    return token_field(jax.random.fold_in(key, 11))


def draw_self_qkv(key, part):
    return projection_weights(jax.random.fold_in(key, 19))


def draw_cross_qkv(key, part):
    return projection_weights(jax.random.fold_in(key, 29))


def steps_of(rng, shape, pieces, least, largest):
    factor_of = 1.0
    for position, shards_of in pieces:
        draws = jax.random.uniform(jax.random.fold_in(jax.random.fold_in(rng, 6), position), (shards_of,), jnp.float32, least / len(pieces), largest / len(pieces))
        factor_of = factor_of * jnp.repeat(jnp.exp(draws), shape[position] // shards_of).reshape((-1,) + (1,) * (len(shape) - 1 - position))
    return factor_of


def gaussian(key, dims, width, reach, shards=(), held_as=jnp.bfloat16):
    entries = jax.random.normal(key, dims, jnp.float32) * width
    if len(shards) > 0:
        entries = steps_of(key, dims, shards, -0.22, 0.18) * entries
    return jnp.clip(entries, min=-reach, max=reach).astype(held_as)


def setup_inputs(seed: int = 0, part: int = 0) -> dict:
    key_of = jax.random.split(jax.random.key(seed), 9)
    part_keys = jax.random.split(jax.random.fold_in(key_of[8], part), 9)
    return {
        "left_tokens": draw_left_tokens(jax.random.fold_in(jax.random.fold_in(key_of[8], part), 71), part),
        "right_tokens": draw_right_tokens(jax.random.fold_in(jax.random.fold_in(key_of[8], part), 71), part),
        "self_qkv": draw_self_qkv(jax.random.fold_in(key_of[8], 71), part),
        "self_out": gaussian(key_of[3], (HEADS * HD, D), (HEADS * HD) ** -0.5, 0.25, ((0, 2),)),
        "cross_qkv": draw_cross_qkv(jax.random.fold_in(key_of[8], 71), part),
        "cross_out": gaussian(key_of[5], (HEADS * HD, D), (HEADS * HD) ** -0.5, 0.25, ((0, 2),)),
        "reassemble": gaussian(key_of[6], (D, CH), D ** -0.5, 0.21875, ((0, 2),)),
        "conv_weight": gaussian(key_of[7], (3, 3, CH, CH), (9 * CH) ** -0.5, 0.125),
    }


def layer_norm(values):
    widened = values.astype(jnp.float32)
    centred = widened - lax.optimization_barrier(jnp.mean(widened, axis=-1, keepdims=True))
    variance = lax.optimization_barrier(jnp.mean(centred * centred, axis=-1, keepdims=True))
    return (centred * lax.rsqrt(variance + 1e-06)).astype(jnp.bfloat16)

def project_rows(normed, weight):
    return jnp.dot(normed, weight, preferred_element_type=jnp.float32).astype(jnp.bfloat16)

def attention(queries, keys_rows, values_rows):
    block_rows = math.gcd(LEN, 512)
    query_blocks = queries.reshape(LEN // block_rows, block_rows, HEADS, HD)
    keys_wide = keys_rows.reshape(LEN, HEADS, HD).astype(jnp.float32)
    values_wide = values_rows.reshape(LEN, HEADS, HD).astype(jnp.float32)

    def one_block(query_block):
        scores = jnp.einsum('qhd,khd->hqk', query_block.astype(jnp.float32), keys_wide) * HD ** (-0.5)
        maxima = lax.optimization_barrier(jnp.max(scores, axis=2, keepdims=True))
        expanded = jnp.exp(scores - maxima)
        totals = lax.optimization_barrier(jnp.sum(expanded, axis=2))
        rounded = lax.optimization_barrier(expanded.astype(jnp.bfloat16)).astype(jnp.float32)
        mixed = jnp.einsum('hqk,khd->qhd', rounded, values_wide)
        return (mixed / totals.T[:, :, None]).reshape(block_rows, HEADS * HD).astype(jnp.bfloat16)
    return lax.map(one_block, query_blocks).reshape(LEN, HEADS * HD)

def one_pair(left_rows, right_rows, self_qkv, self_out, cross_qkv, cross_out, reassemble, conv_weight):
    left_normed = layer_norm(left_rows)
    right_normed = layer_norm(right_rows)
    self_mixed = attention(project_rows(left_normed, self_qkv[0]), project_rows(left_normed, self_qkv[1]), project_rows(left_normed, self_qkv[2]))
    updated = (left_rows.astype(jnp.float32) + jnp.dot(self_mixed, self_out, preferred_element_type=jnp.float32)).astype(jnp.bfloat16)
    updated_normed = layer_norm(updated)
    cross_mixed = attention(project_rows(updated_normed, cross_qkv[0]), project_rows(right_normed, cross_qkv[1]), project_rows(right_normed, cross_qkv[2]))
    final_tokens = (updated.astype(jnp.float32) + jnp.dot(cross_mixed, cross_out, preferred_element_type=jnp.float32)).astype(jnp.bfloat16)
    feature_map = jnp.dot(final_tokens, reassemble, preferred_element_type=jnp.float32).astype(jnp.bfloat16).reshape(GRID_H, GRID_W, CH)
    activated = jnp.maximum(feature_map, jnp.zeros((), jnp.bfloat16))
    padded = jnp.pad(activated, ((1, 1), (1, 1), (0, 0)))
    stacked = jnp.concatenate([padded[row_shift:row_shift + GRID_H, col_shift:col_shift + GRID_W] for row_shift in range(3) for col_shift in range(3)], axis=-1)
    convolved = jnp.dot(stacked.reshape(GRID_H * GRID_W, 9 * CH), conv_weight.reshape(9 * CH, CH), preferred_element_type=jnp.float32)
    return (feature_map.astype(jnp.float32) + convolved.reshape(GRID_H, GRID_W, CH)).astype(jnp.bfloat16)

def reference(left_tokens, right_tokens, self_qkv, self_out, cross_qkv, cross_out, reassemble, conv_weight):
    results = [one_pair(left_tokens[index], right_tokens[index], self_qkv, self_out, cross_qkv, cross_out, reassemble, conv_weight) for index in range(PAIRS)]
    return jnp.stack(results, axis=0)
```

```python
import functools

import jax
import jax.numpy as jnp
from jax import lax
from jax.experimental import pallas as pl
from jax.experimental.pallas import tpu as pltpu
from jax.sharding import PartitionSpec as P

HD = 64
CH = 256
GRID_W = 128
MESH = pl.DeviceIdType.MESH
F32 = jnp.float32
BF16 = jnp.bfloat16


ROWS = 384
CHUNK = 128
NCH = ROWS // CHUNK
FEAT = 384
DIM = 2 * FEAT
COLS = 256
WIN = 80
OUTW = 64

(SW_L, X_L, SW_R, X_R, KS_Z, KS_C, KS_F, KC_Z, KC_C, KC_F, MX, PX, FM) = range(0, 39, 3)
SO, RA, TOP, BOT = 39, 40, 41, 42
N_SEMS = 43

(L_WS, L_WC, L_SO, L_CO, L_RA, L_CW, L_XL, L_XR) = (0, 1, 2, 3, 4, 5, 6, 9)
N_LOCAL = 12


def normalized(a, b):
    mean = (jnp.sum(a, axis=1, keepdims=True) + jnp.sum(b, axis=1, keepdims=True)) * (1.0 / DIM)
    a, b = a - mean, b - mean
    variance = (
        jnp.sum(a * a, axis=1, keepdims=True) + jnp.sum(b * b, axis=1, keepdims=True)
    ) * (1.0 / DIM)
    scale = lax.rsqrt(variance + 1e-06)
    return jnp.concatenate([(a * scale).astype(BF16), (b * scale).astype(BF16)], axis=1)


def fused_kernel(
    lt, rt, ws_h, so_h, wc_h, co_h, ra_h, cw_h, out_ref,
    xl, xr, ws, wc, so, co, ra, cw, qd, kvs, kvc, m_s, l_s, acc_s,
    mixed, upd, w2, part, psend, precv, fms, cin, cf,
    send, recv, local,
):
    g, b, t, p = (lax.axis_index(a) for a in ("groups", "blk", "tile", "pair"))
    half = b // 2
    home = p == half
    guest = p != half
    far = 3 - b
    x_peer = (g, b, 1 - t, p)
    sibling = (g, b, t, 1 - p)
    z_peer = (g, b + 1 - 2 * lax.rem(b, 2), t, p)
    partner = (g, far, t, 1 - p)
    band = jnp.where(home, b, far)
    pair = jnp.where(home, p, 1 - p)

    def rcopy(src, dst, sem, device):
        return pltpu.make_async_remote_copy(
            src_ref=src, dst_ref=dst, send_sem=send.at[sem], recv_sem=recv.at[sem],
            device_id=device, device_id_type=MESH,
        )

    def lcopy(src, dst, sem):
        return pltpu.make_async_copy(src, dst, local.at[sem])

    def rows(c):
        return pl.ds(c * CHUNK, CHUNK)

    def own_local(arg, held, sem, c):
        return lcopy(arg.at[0, rows(c)], held.at[t, rows(c)], sem + c)

    def swap(arg, held, sem, c):
        return rcopy(arg.at[0, rows(c)], held.at[t, rows(c)], sem + c, partner)

    def across(held, sem, c):
        return rcopy(held.at[t, rows(c)], held.at[t, rows(c)], sem + c, x_peer)

    loads = [
        lcopy(ws_h, ws, L_WS),
        lcopy(wc_h, wc, L_WC),
        lcopy(so_h, so.at[t], L_SO),
        lcopy(co_h, co, L_CO),
        lcopy(ra_h, ra.at[t], L_RA),
        lcopy(cw_h, cw, L_CW),
    ]

    @pl.when(home)
    def _():
        for c in range(NCH):
            own_local(lt, xl, L_XL, c).start()

    loads[0].start()
    loads[2].start()

    @pl.when(home)
    def _():
        for c in range(NCH):
            own_local(rt, xr, L_XR, c).start()

    for k in (1, 4, 3, 5):
        loads[k].start()
    cin[...] = jnp.zeros_like(cin)
    qd[...] = jnp.zeros_like(qd)

    barrier = pltpu.get_barrier_semaphore()
    pl.semaphore_signal(barrier, inc=1, device_id=x_peer, device_id_type=MESH)
    pl.semaphore_signal(barrier, inc=1, device_id=sibling, device_id_type=MESH)
    for k in (1, 2, 3):
        for q in range(2):
            pl.semaphore_signal(
                barrier, inc=1, device_id=(g, lax.rem(b + k, 4), t, q), device_id_type=MESH
            )
    pl.semaphore_wait(barrier, 8)

    @pl.when(guest)
    def _():
        for c in range(NCH):
            swap(lt, xl, SW_L, c).start()
        for c in range(NCH):
            swap(rt, xr, SW_R, c).start()

    def forward_tokens(arg, held, l_sem, sw_sem, x_sem):
        for c in range(NCH):

            @pl.when(home)
            def _():
                own_local(arg, held, l_sem, c).wait()

            @pl.when(guest)
            def _():
                swap(arg, held, sw_sem, c).wait_recv()

            across(held, x_sem, c).start()

    forward_tokens(lt, xl, L_XL, SW_L, X_L)
    loads[0].wait()
    loads[2].wait()

    def chunk_normed(held, c):
        return normalized(held[0, rows(c)].astype(F32), held[1, rows(c)].astype(F32))

    def put_query(c, normed, weight):
        q = jnp.dot(normed, weight, preferred_element_type=F32).astype(BF16) * BF16(HD**-0.5)
        qt = q.T
        for hp in range(2):
            qd[c, hp, 0:HD, 0:128] = qt[128 * hp : 128 * hp + HD]
            qd[c, hp, HD:128, 128:256] = qt[128 * hp + HD : 128 * hp + 128]

    def put_keys(kv, c, normed, w_key, w_value):
        k = jnp.dot(normed, w_key, preferred_element_type=F32).astype(BF16)
        v = jnp.dot(normed, w_value, preferred_element_type=F32).astype(BF16).T
        for hp in range(2):
            kv[0, c, hp] = k[:, 128 * hp : 128 * hp + 128]
            kv[0, c, 2 + hp] = v[128 * hp : 128 * hp + 128]

    def to_z(kv, sem, c):
        return rcopy(kv.at[0, c], kv.at[2, c], sem + c, z_peer)

    def to_sibling(kv, sem, c):
        return rcopy(kv.at[0, c], kv.at[1, c], sem + c, sibling)

    def onward(kv, sem, c):
        return rcopy(kv.at[2, c], kv.at[3, c], sem + c, sibling)

    for c in range(NCH):
        across(xl, X_L, c).wait_recv()
        normed = chunk_normed(xl, c)
        put_keys(kvs, c, normed, ws[1], ws[2])
        to_z(kvs, KS_Z, c).start()
        to_sibling(kvs, KS_C, c).start()
        put_query(c, normed, ws[0])

    forward_tokens(rt, xr, L_XR, SW_R, X_R)
    so_copy = rcopy(so.at[t], so.at[t], SO, x_peer)
    so_copy.start()
    loads[4].wait()
    ra_copy = rcopy(ra.at[t], ra.at[t], RA, x_peer)
    ra_copy.start()
    loads[1].wait()

    def flash(kv, slot, c, first):
        for hp in range(2):
            k = kv[slot, :, hp].reshape(ROWS, 128)
            vt = jnp.concatenate([kv[slot, i, 2 + hp] for i in range(NCH)], axis=1)
            s = jnp.dot(k, qd[c, hp], preferred_element_type=F32)
            u = c * 2 + hp
            top = jnp.max(s, axis=0, keepdims=True)
            if not first:
                old = m_s[u]
                top = jnp.maximum(old, top)
            e = jnp.exp(s - top)
            total = jnp.sum(e, axis=0, keepdims=True)
            pv = jnp.dot(vt, e.astype(BF16), preferred_element_type=F32)
            upper, lower = pv[0:HD, 0:128], pv[HD:128, 128:256]
            if not first:
                fix = jnp.exp(old - top)
                total = total + l_s[u] * fix
                upper = upper + acc_s[u, 0:HD] * fix[:, 0:128]
                lower = lower + acc_s[u, HD:128] * fix[:, 128:256]
            m_s[u] = top
            l_s[u] = total
            acc_s[u, 0:HD] = upper
            acc_s[u, HD:128] = lower

    def flash_rows(kv, slot, first):
        def one(c, carry):
            flash(kv, slot, c, first)
            return carry

        lax.fori_loop(0, NCH, one, 0)

    def finished(c):
        parts = []
        for hp in range(2):
            u = c * 2 + hp
            total = l_s[u]
            o = jnp.concatenate(
                [acc_s[u, 0:HD] / total[:, 0:128], acc_s[u, HD:128] / total[:, 128:256]], axis=0
            )
            parts.append(o.T.astype(BF16))
        return jnp.concatenate(parts, axis=1)

    flash_rows(kvs, 0, True)
    for c in range(NCH):
        to_sibling(kvs, KS_C, c).wait_recv()
    flash_rows(kvs, 1, False)
    for c in range(NCH):
        to_z(kvs, KS_Z, c).wait_recv()
        onward(kvs, KS_F, c).start()

    for c in range(NCH):
        across(xr, X_R, c).wait_recv()
        normed = chunk_normed(xr, c)
        put_keys(kvc, c, normed, wc[1], wc[2])
        to_z(kvc, KC_Z, c).start()
        to_sibling(kvc, KC_C, c).start()

    flash_rows(kvs, 2, False)
    for c in range(NCH):
        onward(kvs, KS_F, c).wait_recv()

    def mixed_across(c):
        return rcopy(mixed.at[t, rows(c)], mixed.at[t, rows(c)], MX + c, x_peer)

    for c in range(NCH):
        flash(kvs, 3, c, False)
        mixed[t, rows(c)] = finished(c)
        mixed_across(c).start()

    so_copy.wait_recv()
    for c in range(NCH):
        mixed_across(c).wait_recv()
        both = jnp.concatenate([mixed[0, rows(c)], mixed[1, rows(c)]], axis=1)
        term = jnp.dot(both, so[...].reshape(2 * COLS, DIM), preferred_element_type=F32)
        a = (xl[0, rows(c)].astype(F32) + term[:, :FEAT]).astype(BF16)
        d = (xl[1, rows(c)].astype(F32) + term[:, FEAT:]).astype(BF16)
        upd[rows(c), 0:FEAT] = a
        upd[rows(c), FEAT:DIM] = d
        put_query(c, normalized(a.astype(F32), d.astype(F32)), wc[0])

    flash_rows(kvc, 0, True)
    for c in range(NCH):
        to_sibling(kvc, KC_C, c).wait_recv()
    flash_rows(kvc, 1, False)
    loads[3].wait()
    ra_copy.wait_recv()
    w2[...] = jnp.dot(co[...], ra[...].reshape(DIM, CH), preferred_element_type=F32).astype(BF16)
    for c in range(NCH):
        to_z(kvc, KC_Z, c).wait_recv()
        onward(kvc, KC_F, c).start()
    flash_rows(kvc, 2, False)
    for c in range(NCH):
        onward(kvc, KC_F, c).wait_recv()

    def partial_across(c):
        return rcopy(psend.at[c], precv.at[c], PX + c, x_peer)

    for c in range(NCH):
        flash(kvc, 3, c, False)
        part[c] = jnp.dot(finished(c), w2[...], preferred_element_type=F32)
        theirs = pl.ds(pl.multiple_of(48 * (1 - t), 16), WIN)
        psend[c] = part[c, theirs].astype(BF16)
        partial_across(c).start()

    place = pl.ds(pl.multiple_of(16 * (1 - t), 16), WIN)

    def map_home(c):
        return rcopy(fms.at[c], cin.at[1 + c, place], FM + c, partner)

    def map_above():
        return rcopy(fms.at[0], cin.at[4, place], TOP, (g, band - 1, t, pair))

    def map_below():
        return rcopy(fms.at[NCH - 1], cin.at[0, place], BOT, (g, band + 1, t, pair))

    for c in range(NCH):
        mine = pl.ds(pl.multiple_of(48 * t, 16), WIN)
        tokens = upd[pl.ds(pl.multiple_of(c * CHUNK + 48 * t, 16), WIN)]
        base = jnp.dot(tokens, ra[...].reshape(DIM, CH), preferred_element_type=F32)
        base = base + part[c, mine]
        partial_across(c).wait_recv()
        row = (base + precv[c].astype(F32)).astype(BF16)
        fms[c] = row

        @pl.when(guest)
        def _():
            map_home(c).start()

        @pl.when(home)
        def _():
            cin[1 + c, place] = row

        if c == 0:

            @pl.when(band > 0)
            def _():
                map_above().start()

        if c == NCH - 1:

            @pl.when(band < 3)
            def _():
                map_below().start()

    loads[5].wait()

    @pl.when(guest)
    def _():
        for c in range(NCH):
            map_home(c).wait_recv()

    @pl.when(b < 3)
    def _():
        map_above().wait_recv()

    @pl.when(b > 0)
    def _():
        map_below().wait_recv()

    cf[...] = jnp.maximum(cin[...].astype(F32), 0.0)
    shifted = jnp.concatenate(
        [
            cf[:, 15 + s : 15 + s + OUTW].astype(BF16).reshape((NCH + 2) * OUTW, CH)
            for s in range(3)
        ],
        axis=1,
    )
    total = cin[1 : 1 + NCH, 16 : 16 + OUTW].astype(F32).reshape(NCH * OUTW, CH)
    for a in range(3):
        total = total + jnp.dot(
            shifted[a * OUTW : (a + NCH) * OUTW],
            cw[a].reshape(3 * CH, CH),
            preferred_element_type=F32,
        )
    out_ref[0] = total.astype(BF16).reshape(NCH, OUTW, CH)

    @pl.when(guest)
    def _():
        for c in range(NCH):
            swap(lt, xl, SW_L, c).wait_send()
            swap(rt, xr, SW_R, c).wait_send()
            map_home(c).wait_send()

    for c in range(NCH):
        across(xl, X_L, c).wait_send()
        across(xr, X_R, c).wait_send()
        for kv, z_sem, c_sem, f_sem in ((kvs, KS_Z, KS_C, KS_F), (kvc, KC_Z, KC_C, KC_F)):
            to_z(kv, z_sem, c).wait_send()
            to_sibling(kv, c_sem, c).wait_send()
            onward(kv, f_sem, c).wait_send()
        mixed_across(c).wait_send()
        partial_across(c).wait_send()
    so_copy.wait_send()
    ra_copy.wait_send()

    @pl.when(band > 0)
    def _():
        map_above().wait_send()

    @pl.when(band < 3)
    def _():
        map_below().wait_send()


def fused_body(*arrays):
    hbm = pl.BlockSpec(memory_space=pl.ANY)
    return pl.pallas_call(
        fused_kernel,
        out_shape=jax.ShapeDtypeStruct((1, NCH, OUTW, CH), BF16),
        in_specs=[hbm] * len(arrays),
        out_specs=pl.BlockSpec(memory_space=pltpu.VMEM),
        scratch_shapes=[
            pltpu.VMEM((2, ROWS, FEAT), BF16),
            pltpu.VMEM((2, ROWS, FEAT), BF16),
            pltpu.VMEM((3, DIM, COLS), BF16),
            pltpu.VMEM((3, DIM, COLS), BF16),
            pltpu.VMEM((2, COLS, DIM), BF16),
            pltpu.VMEM((COLS, DIM), BF16),
            pltpu.VMEM((2, FEAT, CH), BF16),
            pltpu.VMEM((3, 3, CH, CH), BF16),
            pltpu.VMEM((NCH, 2, 128, 256), BF16),
            pltpu.VMEM((4, NCH, 4, 128, 128), BF16),
            pltpu.VMEM((4, NCH, 4, 128, 128), BF16),
            pltpu.VMEM((2 * NCH, 1, 256), F32),
            pltpu.VMEM((2 * NCH, 1, 256), F32),
            pltpu.VMEM((2 * NCH, 128, 128), F32),
            pltpu.VMEM((2, ROWS, COLS), BF16),
            pltpu.VMEM((ROWS, DIM), BF16),
            pltpu.VMEM((COLS, CH), BF16),
            pltpu.VMEM((NCH, CHUNK, CH), F32),
            pltpu.VMEM((NCH, WIN, CH), BF16),
            pltpu.VMEM((NCH, WIN, CH), BF16),
            pltpu.VMEM((NCH, WIN, CH), BF16),
            pltpu.VMEM((NCH + 2, 96, CH), BF16),
            pltpu.VMEM((NCH + 2, 96, CH), F32),
            pltpu.SemaphoreType.DMA((N_SEMS,)),
            pltpu.SemaphoreType.DMA((N_SEMS,)),
            pltpu.SemaphoreType.DMA((N_LOCAL,)),
        ],
        compiler_params=pltpu.CompilerParams(
            collective_id=0, has_side_effects=True, vmem_limit_bytes=56 * 2**20
        ),
        cost_estimate=pl.CostEstimate(
            flops=3 * 10**9, bytes_accessed=6 * 10**6, transcendentals=5 * 10**6
        ),
        name="decoder",
    )(*arrays)


def layer_norm(values):
    widened = values.astype(F32)
    centred = widened - jnp.mean(widened, axis=-1, keepdims=True)
    variance = jnp.mean(centred * centred, axis=-1, keepdims=True)
    return (centred * lax.rsqrt(variance + 1e-06)).astype(BF16)


def project_rows(normed, weight):
    return jnp.dot(normed, weight, preferred_element_type=F32).astype(BF16)


def attend_keys(running, queries, keys_rows, values_rows):
    maxima, totals, accumulated = running
    query_count = queries.shape[0]
    head_count = queries.shape[1] // HD
    key_count = keys_rows.shape[0]
    scores = jnp.einsum(
        "qhd,khd->hqk",
        queries.reshape(query_count, head_count, HD),
        keys_rows.reshape(key_count, head_count, HD),
        preferred_element_type=F32,
    ) * HD ** (-0.5)
    new_maxima = jnp.maximum(maxima, jnp.max(scores, axis=2))
    correction = jnp.exp(maxima - new_maxima)
    expanded = jnp.exp(scores - new_maxima[:, :, None])
    totals = totals * correction + jnp.sum(expanded, axis=2)
    mixed = jnp.einsum(
        "hqk,khd->qhd",
        expanded.astype(BF16),
        values_rows.reshape(key_count, head_count, HD),
        preferred_element_type=F32,
    )
    accumulated = (
        accumulated.reshape(query_count, head_count, HD) * correction.T[:, :, None] + mixed
    )
    return (new_maxima, totals, accumulated.reshape(query_count, head_count * HD))


def attention_over(queries, pieces):
    query_count = queries.shape[0]
    head_count = queries.shape[1] // HD
    running = (
        jnp.full((head_count, query_count), -jnp.inf, F32),
        jnp.zeros((head_count, query_count), F32),
        jnp.zeros(queries.shape, F32),
    )
    for piece in pieces:
        running = attend_keys(running, queries, piece[0], piece[1])
    maxima, totals, accumulated = running
    normalized_rows = accumulated.reshape(query_count, head_count, HD) / totals.T[:, :, None]
    return normalized_rows.reshape(query_count, head_count * HD).astype(BF16)


def shifted_pieces(value, axis):
    count = lax.axis_size(axis)
    return [value] + [
        lax.ppermute(value, axis, [(i, (i + shift) % count) for i in range(count)])
        for shift in range(1, count)
    ]


def gather_columns(value, axis):
    count = lax.axis_size(axis)
    index = lax.axis_index(axis)
    width = value.shape[-1]
    whole = jnp.zeros(value.shape[:-1] + (count * width,), value.dtype)
    for shift, piece in enumerate(shifted_pieces(value, axis)):
        start = lax.rem(index - shift + count, count) * width
        whole = lax.dynamic_update_slice_in_dim(whole, piece, start, axis=value.ndim - 1)
    return whole


def sum_over(value, axis):
    total = value.astype(F32)
    for piece in shifted_pieces(value, axis)[1:]:
        total = total + piece.astype(F32)
    return total


def with_border_rows(cells):
    count = lax.axis_size("blk")
    up = [(i, i + 1) for i in range(count - 1)]
    down = [(i + 1, i) for i in range(count - 1)]
    return jnp.concatenate(
        [lax.ppermute(cells[-1:], "blk", up), cells, lax.ppermute(cells[:1], "blk", down)], axis=0
    )


def general_body(
    left_tokens, right_tokens, self_qkv, self_out, cross_qkv, cross_out, reassemble, conv_weight
):
    tiles = lax.axis_size("tile")
    tile_index = lax.axis_index("tile")
    token_count = left_tokens.shape[1]
    left_full = gather_columns(left_tokens[0], "tile")
    right_full = gather_columns(right_tokens[0], "tile")
    reassemble_full = gather_columns(reassemble.T, "tile").T
    left_normed = layer_norm(left_full)
    right_normed = layer_norm(right_full)
    self_query = project_rows(left_normed, self_qkv[0])
    self_pieces = shifted_pieces(
        jnp.stack([project_rows(left_normed, self_qkv[1]), project_rows(left_normed, self_qkv[2])]),
        "blk",
    )
    cross_pieces = shifted_pieces(
        jnp.stack(
            [project_rows(right_normed, cross_qkv[1]), project_rows(right_normed, cross_qkv[2])]
        ),
        "blk",
    )
    self_mixed = attention_over(self_query, self_pieces)
    self_term = jnp.dot(self_mixed, self_out, preferred_element_type=F32)
    self_sum = sum_over(self_term.astype(BF16), "tile")
    updated = (left_full.astype(F32) + self_sum).astype(BF16)
    cross_query = project_rows(layer_norm(updated), cross_qkv[0])
    cross_mixed = attention_over(cross_query, cross_pieces)
    cross_term = jnp.dot(cross_mixed, cross_out, preferred_element_type=F32)
    cross_sum = sum_over(cross_term.astype(BF16), "tile")
    final_tokens = (updated.astype(F32) + cross_sum).astype(BF16)
    band_rows = token_count // GRID_W
    column_count = GRID_W // tiles
    grid = jnp.pad(final_tokens.reshape(band_rows, GRID_W, -1), ((0, 0), (1, 1), (0, 0)))
    window = lax.dynamic_slice_in_dim(grid, tile_index * column_count, column_count + 2, axis=1)
    wide_map = jnp.dot(
        window.reshape(band_rows * (column_count + 2), -1),
        reassemble_full,
        preferred_element_type=F32,
    )
    wide_map = wide_map.astype(BF16).reshape(band_rows, column_count + 2, CH)
    feature_map = wide_map[:, 1 : column_count + 1]
    padded = with_border_rows(jnp.maximum(wide_map, jnp.zeros((), BF16)))
    stacked = jnp.concatenate(
        [
            padded[row_shift : row_shift + band_rows, col_shift : col_shift + column_count]
            for row_shift in range(3)
            for col_shift in range(3)
        ],
        axis=-1,
    )
    convolved = jnp.dot(
        stacked.reshape(band_rows * column_count, 9 * CH),
        conv_weight.reshape(9 * CH, CH),
        preferred_element_type=F32,
    )
    joined = feature_map.astype(F32) + convolved.reshape(band_rows, column_count, CH)
    return joined.astype(BF16)[None]


def whole_program(mesh, *arrays):
    shape = mesh.shape
    left, qkv = arrays[0], arrays[2]
    fits = (
        shape["blk"] == 4
        and shape["tile"] == 2
        and shape["pair"] == 2
        and left.shape[0] == 2 * shape["groups"]
        and left.shape[1] == 4 * ROWS
        and left.shape[2] == DIM
        and qkv.shape[2] == 2 * COLS
    )
    placed = (
        P(("groups", "pair"), "blk", "tile"),
        P(("groups", "pair"), "blk", "tile"),
        P(None, None, "tile"),
        P("tile", None),
        P(None, None, "tile"),
        P("tile", None),
        P("tile", None),
        P(),
    )
    return jax.shard_map(
        fused_body if fits else general_body,
        mesh=mesh,
        in_specs=placed,
        out_specs=P(("groups", "pair"), "blk", "tile", None),
        check_vma=False,
    )(*arrays)


def solution(mesh):
    return functools.partial(whole_program, mesh)
```

```python
import functools

import jax
import jax.numpy as jnp
from jax import lax
from jax.experimental import pallas as pl
from jax.experimental.pallas import tpu as pltpu
from jax.sharding import PartitionSpec as P

HD = 64
CH = 256
GRID_W = 128
MESH = pl.DeviceIdType.MESH
F32 = jnp.float32
BF16 = jnp.bfloat16


ROWS = 384
CHUNK = 128
NCH = ROWS // CHUNK
FEAT = 384
DIM = 2 * FEAT
COLS = 256
WIN = 80
OUTW = 64

(SW_L, X_L, SW_R, X_R, KS_Z, KS_C, KS_F, KC_Z, KC_C, KC_F, MX, PX, FM) = range(0, 39, 3)
TOP, BOT = 39, 40
SO, RA = 41, 45
N_SEMS = 49

(L_WS, L_WC, L_SO, L_CO, L_RA, L_CW, L_XL, L_XR) = (0, 1, 2, 3, 4, 5, 6, 9)
N_LOCAL = 12


def normalized(a, b):
    mean = (jnp.sum(a, axis=1, keepdims=True) + jnp.sum(b, axis=1, keepdims=True)) * (1.0 / DIM)
    a, b = a - mean, b - mean
    variance = (
        jnp.sum(a * a, axis=1, keepdims=True) + jnp.sum(b * b, axis=1, keepdims=True)
    ) * (1.0 / DIM)
    scale = lax.rsqrt(variance + 1e-06)
    return jnp.concatenate([(a * scale).astype(BF16), (b * scale).astype(BF16)], axis=1)


def fused_kernel(
    lt, rt, ws_h, so_h, wc_h, co_h, ra_h, cw_h, out_ref,
    xl, xr, ws, wc, so, co, ra, cw, qd, kvs, kvc, m_s, l_s, acc_s,
    mixed, upd, w2, part, psend, precv, fms, cin, cf,
    send, recv, local,
):
    g, b, t, p = (lax.axis_index(a) for a in ("groups", "blk", "tile", "pair"))
    half = b // 2
    home = p == half
    guest = p != half
    far = 3 - b
    x_peer = (g, b, 1 - t, p)
    sibling = (g, b, t, 1 - p)
    z_peer = (g, b + 1 - 2 * lax.rem(b, 2), t, p)
    partner = (g, far, t, 1 - p)
    band = jnp.where(home, b, far)
    pair = jnp.where(home, p, 1 - p)

    def rcopy(src, dst, sem, device):
        return pltpu.make_async_remote_copy(
            src_ref=src, dst_ref=dst, send_sem=send.at[sem], recv_sem=recv.at[sem],
            device_id=device, device_id_type=MESH,
        )

    def lcopy(src, dst, sem):
        return pltpu.make_async_copy(src, dst, local.at[sem])

    def rows(c):
        return pl.ds(c * CHUNK, CHUNK)

    def own_local(arg, held, sem, c):
        return lcopy(arg.at[0, rows(c)], held.at[t, rows(c)], sem + c)

    def swap(arg, held, sem, c):
        return rcopy(arg.at[0, rows(c)], held.at[t, rows(c)], sem + c, partner)

    def across(held, sem, c):
        return rcopy(held.at[t, rows(c)], held.at[t, rows(c)], sem + c, x_peer)

    loads = [
        lcopy(ws_h, ws, L_WS),
        lcopy(wc_h, wc, L_WC),
        lcopy(so_h, so.at[t], L_SO),
        lcopy(co_h, co, L_CO),
        lcopy(ra_h, ra.at[t], L_RA),
        lcopy(cw_h, cw, L_CW),
    ]

    @pl.when(home)
    def _():
        for c in range(NCH):
            own_local(lt, xl, L_XL, c).start()

    loads[0].start()
    loads[2].start()

    @pl.when(home)
    def _():
        for c in range(NCH):
            own_local(rt, xr, L_XR, c).start()

    for k in (1, 4, 3, 5):
        loads[k].start()
    cin[...] = jnp.zeros_like(cin)
    qd[...] = jnp.zeros_like(qd)

    y_peer = (1 - g, b, t, p)

    barrier = pltpu.get_barrier_semaphore()
    pl.semaphore_signal(barrier, inc=1, device_id=y_peer, device_id_type=MESH)
    pl.semaphore_signal(barrier, inc=1, device_id=x_peer, device_id_type=MESH)
    pl.semaphore_signal(barrier, inc=1, device_id=sibling, device_id_type=MESH)
    for k in (1, 2, 3):
        for q in range(2):
            pl.semaphore_signal(
                barrier, inc=1, device_id=(g, lax.rem(b + k, 4), t, q), device_id_type=MESH
            )
    pl.semaphore_wait(barrier, 9)

    @pl.when(guest)
    def _():
        for c in range(NCH):
            swap(lt, xl, SW_L, c).start()
        for c in range(NCH):
            swap(rt, xr, SW_R, c).start()

    def forward_home(arg, held, l_sem, x_sem):
        @pl.when(home)
        def _():
            for c in range(NCH):
                own_local(arg, held, l_sem, c).wait()
                across(held, x_sem, c).start()

    def forward_guest(arg, held, sw_sem, x_sem):
        @pl.when(guest)
        def _():
            for c in range(NCH):
                swap(arg, held, sw_sem, c).wait_recv()
                across(held, x_sem, c).start()

    forward_home(lt, xl, L_XL, X_L)
    forward_guest(lt, xl, SW_L, X_L)

    loads[0].wait()

    def chunk_normed(held, c):
        return normalized(held[0, rows(c)].astype(F32), held[1, rows(c)].astype(F32))

    def put_query(c, normed, weight):
        q = jnp.dot(normed, weight, preferred_element_type=F32).astype(BF16) * BF16(HD**-0.5)
        qt = q.T
        for hp in range(2):
            qd[c, hp, 0:HD, 0:128] = qt[128 * hp : 128 * hp + HD]
            qd[c, hp, HD:128, 128:256] = qt[128 * hp + HD : 128 * hp + 128]

    def put_keys(kv, c, normed, w_key, w_value):
        k = jnp.dot(normed, w_key, preferred_element_type=F32).astype(BF16)
        v = jnp.dot(normed, w_value, preferred_element_type=F32).astype(BF16).T
        for hp in range(2):
            kv[0, c, hp] = k[:, 128 * hp : 128 * hp + 128]
            kv[0, c, 2 + hp] = v[128 * hp : 128 * hp + 128]

    def to_z(kv, sem, c):
        return rcopy(kv.at[0, c], kv.at[2, c], sem + c, z_peer)

    def to_sibling(kv, sem, c):
        return rcopy(kv.at[0, c], kv.at[1, c], sem + c, sibling)

    def onward(kv, sem, c):
        return rcopy(kv.at[2, c], kv.at[3, c], sem + c, sibling)

    for c in range(NCH):
        across(xl, X_L, c).wait_recv()
        normed = chunk_normed(xl, c)
        put_keys(kvs, c, normed, ws[1], ws[2])
        to_z(kvs, KS_Z, c).start()
        to_sibling(kvs, KS_C, c).start()
        put_query(c, normed, ws[0])

    forward_home(rt, xr, L_XR, X_R)
    forward_guest(rt, xr, SW_R, X_R)

    class Shared:
        def __init__(self, ref, sem):
            self.ref, self.sem, self.size = ref, sem, ref.shape[1] // 4

        def copy(self, side, quarter, k, device):
            at = pl.ds(pl.multiple_of(quarter * self.size, self.size), self.size)
            return rcopy(self.ref.at[side, at], self.ref.at[side, at], self.sem + k, device)

        def over_tile(self):
            return self.copy(t, 2 * g + p, 0, x_peer)

        def over_groups(self):
            return self.copy(1 - t, 2 * g + p, 1, y_peer)

        def to_core(self):
            return self.copy(1 - t, 2 * g + p, 2, sibling)

        def to_core_later(self):
            return self.copy(1 - t, 2 * (1 - g) + p, 3, sibling)

        def pass_on(self):
            self.over_tile().wait_recv()
            self.over_groups().start()
            self.to_core().start()

        def pass_on_later(self):
            self.over_groups().wait_recv()
            self.to_core_later().start()

        def wait_recv(self):
            self.to_core().wait_recv()
            self.to_core_later().wait_recv()

        def wait_send(self):
            self.over_tile().wait_send()
            self.over_groups().wait_send()
            self.to_core().wait_send()
            self.to_core_later().wait_send()

    so_copy, ra_copy = Shared(so, SO), Shared(ra, RA)
    loads[2].wait()
    so_copy.over_tile().start()
    loads[4].wait()
    ra_copy.over_tile().start()
    loads[1].wait()

    def flash(kv, slot, chunks, first):
        units = [(c, hp) for c in chunks for hp in range(2)]
        keys = [kv[slot, :, hp].reshape(ROWS, 128) for hp in range(2)]
        values = [
            jnp.concatenate([kv[slot, i, 2 + hp] for i in range(NCH)], axis=1) for hp in range(2)
        ]
        scores = [jnp.dot(keys[hp], qd[c, hp], preferred_element_type=F32) for c, hp in units]
        if not first:
            held = [(m_s[2 * c + hp], l_s[2 * c + hp], acc_s[2 * c + hp]) for c, hp in units]
        results = []
        for i, (c, hp) in enumerate(units):
            top = jnp.max(scores[i], axis=0, keepdims=True)
            if not first:
                top = jnp.maximum(held[i][0], top)
            e = jnp.exp(scores[i] - top)
            total = jnp.sum(e, axis=0, keepdims=True)
            pv = jnp.dot(values[hp], e.astype(BF16), preferred_element_type=F32)
            upper, lower = pv[0:HD, 0:128], pv[HD:128, 128:256]
            if not first:
                fix = jnp.exp(held[i][0] - top)
                total = total + held[i][1] * fix
                upper = upper + held[i][2][0:HD] * fix[:, 0:128]
                lower = lower + held[i][2][HD:128] * fix[:, 128:256]
            results.append((top, total, upper, lower))
        for i, (c, hp) in enumerate(units):
            u = c * 2 + hp
            m_s[u], l_s[u], acc_s[u, 0:HD], acc_s[u, HD:128] = results[i]

    def slot_of(step):
        return jnp.where(home, (0, 2, 1, 3)[step], (0, 1, 3, 2)[step])

    def from_z(kv, z_sem, f_sem):
        for c in range(NCH):
            to_z(kv, z_sem, c).wait_recv()
            onward(kv, f_sem, c).start()

    def arrive(kv, step, z_sem, c_sem, f_sem):
        @pl.when(home)
        def _():
            if step == 1:
                from_z(kv, z_sem, f_sem)
            for c in range(NCH):
                if step == 2:
                    to_sibling(kv, c_sem, c).wait_recv()
                if step == 3:
                    onward(kv, f_sem, c).wait_recv()

        @pl.when(guest)
        def _():
            if step == 3:
                from_z(kv, z_sem, f_sem)
            for c in range(NCH):
                if step == 1:
                    to_sibling(kv, c_sem, c).wait_recv()
                if step == 2:
                    onward(kv, f_sem, c).wait_recv()

    def finished(c):
        parts = []
        for hp in range(2):
            u = c * 2 + hp
            total = l_s[u]
            o = jnp.concatenate(
                [acc_s[u, 0:HD] / total[:, 0:128], acc_s[u, HD:128] / total[:, 128:256]], axis=0
            )
            parts.append(o.T.astype(BF16))
        return jnp.concatenate(parts, axis=1)

    every = range(NCH)
    self_sems, cross_sems = (KS_Z, KS_C, KS_F), (KC_Z, KC_C, KC_F)
    flash(kvs, 0, every, True)
    arrive(kvs, 1, *self_sems)
    flash(kvs, slot_of(1), every, False)
    arrive(kvs, 2, *self_sems)
    flash(kvs, slot_of(2), every, False)
    arrive(kvs, 3, *self_sems)

    for c in range(NCH):
        across(xr, X_R, c).wait_recv()
        normed = chunk_normed(xr, c)
        put_keys(kvc, c, normed, wc[1], wc[2])
        to_z(kvc, KC_Z, c).start()
        to_sibling(kvc, KC_C, c).start()

    so_copy.pass_on()
    ra_copy.pass_on()

    def mixed_across(c):
        return rcopy(mixed.at[t, rows(c)], mixed.at[t, rows(c)], MX + c, x_peer)

    for c in range(NCH):
        flash(kvs, slot_of(3), [c], False)
        mixed[t, rows(c)] = finished(c)
        mixed_across(c).start()

    so_copy.pass_on_later()
    ra_copy.pass_on_later()
    so_copy.wait_recv()
    for c in range(NCH):
        mixed_across(c).wait_recv()
        both = jnp.concatenate([mixed[0, rows(c)], mixed[1, rows(c)]], axis=1)
        term = jnp.dot(both, so[...].reshape(2 * COLS, DIM), preferred_element_type=F32)
        a = (xl[0, rows(c)].astype(F32) + term[:, :FEAT]).astype(BF16)
        d = (xl[1, rows(c)].astype(F32) + term[:, FEAT:]).astype(BF16)
        upd[rows(c), 0:FEAT] = a
        upd[rows(c), FEAT:DIM] = d
        put_query(c, normalized(a.astype(F32), d.astype(F32)), wc[0])

    flash(kvc, 0, every, True)
    arrive(kvc, 1, *cross_sems)
    flash(kvc, slot_of(1), every, False)
    loads[3].wait()
    ra_copy.wait_recv()
    w2[...] = jnp.dot(co[...], ra[...].reshape(DIM, CH), preferred_element_type=F32).astype(BF16)
    arrive(kvc, 2, *cross_sems)
    flash(kvc, slot_of(2), every, False)
    arrive(kvc, 3, *cross_sems)

    def partial_across(c):
        return rcopy(psend.at[c], precv.at[c], PX + c, x_peer)

    for c in range(NCH):
        flash(kvc, slot_of(3), [c], False)
        part[c] = jnp.dot(finished(c), w2[...], preferred_element_type=F32)
        theirs = pl.ds(pl.multiple_of(48 * (1 - t), 16), WIN)
        psend[c] = part[c, theirs].astype(BF16)
        partial_across(c).start()

    place = pl.ds(pl.multiple_of(16 * (1 - t), 16), WIN)

    def map_home(c):
        return rcopy(fms.at[c], cin.at[1 + c, place], FM + c, partner)

    def map_above():
        return rcopy(fms.at[0], cin.at[4, place], TOP, (g, band - 1, t, pair))

    def map_below():
        return rcopy(fms.at[NCH - 1], cin.at[0, place], BOT, (g, band + 1, t, pair))

    for c in range(NCH):
        mine = pl.ds(pl.multiple_of(48 * t, 16), WIN)
        tokens = upd[pl.ds(pl.multiple_of(c * CHUNK + 48 * t, 16), WIN)]
        base = jnp.dot(tokens, ra[...].reshape(DIM, CH), preferred_element_type=F32)
        base = base + part[c, mine]
        partial_across(c).wait_recv()
        row = (base + precv[c].astype(F32)).astype(BF16)
        fms[c] = row

        @pl.when(guest)
        def _():
            map_home(c).start()

        @pl.when(home)
        def _():
            cin[1 + c, place] = row

        if c == 0:

            @pl.when(band > 0)
            def _():
                map_above().start()

        if c == NCH - 1:

            @pl.when(band < 3)
            def _():
                map_below().start()

    loads[5].wait()

    @pl.when(guest)
    def _():
        for c in range(NCH):
            map_home(c).wait_recv()

    @pl.when(b < 3)
    def _():
        map_above().wait_recv()

    @pl.when(b > 0)
    def _():
        map_below().wait_recv()

    cf[...] = jnp.maximum(cin[...].astype(F32), 0.0)
    shifted = jnp.concatenate(
        [
            cf[:, 15 + s : 15 + s + OUTW].astype(BF16).reshape((NCH + 2) * OUTW, CH)
            for s in range(3)
        ],
        axis=1,
    )
    total = cin[1 : 1 + NCH, 16 : 16 + OUTW].astype(F32).reshape(NCH * OUTW, CH)
    for a in range(3):
        total = total + jnp.dot(
            shifted[a * OUTW : (a + NCH) * OUTW],
            cw[a].reshape(3 * CH, CH),
            preferred_element_type=F32,
        )
    out_ref[0] = total.astype(BF16).reshape(NCH, OUTW, CH)

    @pl.when(guest)
    def _():
        for c in range(NCH):
            swap(lt, xl, SW_L, c).wait_send()
            swap(rt, xr, SW_R, c).wait_send()
            map_home(c).wait_send()

    for c in range(NCH):
        across(xl, X_L, c).wait_send()
        across(xr, X_R, c).wait_send()
        for kv, z_sem, c_sem, f_sem in ((kvs, KS_Z, KS_C, KS_F), (kvc, KC_Z, KC_C, KC_F)):
            to_z(kv, z_sem, c).wait_send()
            to_sibling(kv, c_sem, c).wait_send()
            onward(kv, f_sem, c).wait_send()
        mixed_across(c).wait_send()
        partial_across(c).wait_send()
    so_copy.wait_send()
    ra_copy.wait_send()

    @pl.when(band > 0)
    def _():
        map_above().wait_send()

    @pl.when(band < 3)
    def _():
        map_below().wait_send()


def fused_body(*arrays):
    hbm = pl.BlockSpec(memory_space=pl.ANY)
    return pl.pallas_call(
        fused_kernel,
        out_shape=jax.ShapeDtypeStruct((1, NCH, OUTW, CH), BF16),
        in_specs=[hbm] * len(arrays),
        out_specs=pl.BlockSpec(memory_space=pltpu.VMEM),
        scratch_shapes=[
            pltpu.VMEM((2, ROWS, FEAT), BF16),
            pltpu.VMEM((2, ROWS, FEAT), BF16),
            pltpu.VMEM((3, DIM, COLS), BF16),
            pltpu.VMEM((3, DIM, COLS), BF16),
            pltpu.VMEM((2, COLS, DIM), BF16),
            pltpu.VMEM((COLS, DIM), BF16),
            pltpu.VMEM((2, FEAT, CH), BF16),
            pltpu.VMEM((3, 3, CH, CH), BF16),
            pltpu.VMEM((NCH, 2, 128, 256), BF16),
            pltpu.VMEM((4, NCH, 4, 128, 128), BF16),
            pltpu.VMEM((4, NCH, 4, 128, 128), BF16),
            pltpu.VMEM((2 * NCH, 1, 256), F32),
            pltpu.VMEM((2 * NCH, 1, 256), F32),
            pltpu.VMEM((2 * NCH, 128, 128), F32),
            pltpu.VMEM((2, ROWS, COLS), BF16),
            pltpu.VMEM((ROWS, DIM), BF16),
            pltpu.VMEM((COLS, CH), BF16),
            pltpu.VMEM((NCH, CHUNK, CH), F32),
            pltpu.VMEM((NCH, WIN, CH), BF16),
            pltpu.VMEM((NCH, WIN, CH), BF16),
            pltpu.VMEM((NCH, WIN, CH), BF16),
            pltpu.VMEM((NCH + 2, 96, CH), BF16),
            pltpu.VMEM((NCH + 2, 96, CH), F32),
            pltpu.SemaphoreType.DMA((N_SEMS,)),
            pltpu.SemaphoreType.DMA((N_SEMS,)),
            pltpu.SemaphoreType.DMA((N_LOCAL,)),
        ],
        compiler_params=pltpu.CompilerParams(
            collective_id=0, has_side_effects=True, vmem_limit_bytes=56 * 2**20
        ),
        cost_estimate=pl.CostEstimate(
            flops=3 * 10**9, bytes_accessed=6 * 10**6, transcendentals=5 * 10**6
        ),
        name="decoder",
    )(*arrays)


def layer_norm(values):
    widened = values.astype(F32)
    centred = widened - jnp.mean(widened, axis=-1, keepdims=True)
    variance = jnp.mean(centred * centred, axis=-1, keepdims=True)
    return (centred * lax.rsqrt(variance + 1e-06)).astype(BF16)


def project_rows(normed, weight):
    return jnp.dot(normed, weight, preferred_element_type=F32).astype(BF16)


def attend_keys(running, queries, keys_rows, values_rows):
    maxima, totals, accumulated = running
    query_count = queries.shape[0]
    head_count = queries.shape[1] // HD
    key_count = keys_rows.shape[0]
    scores = jnp.einsum(
        "qhd,khd->hqk",
        queries.reshape(query_count, head_count, HD),
        keys_rows.reshape(key_count, head_count, HD),
        preferred_element_type=F32,
    ) * HD ** (-0.5)
    new_maxima = jnp.maximum(maxima, jnp.max(scores, axis=2))
    correction = jnp.exp(maxima - new_maxima)
    expanded = jnp.exp(scores - new_maxima[:, :, None])
    totals = totals * correction + jnp.sum(expanded, axis=2)
    mixed = jnp.einsum(
        "hqk,khd->qhd",
        expanded.astype(BF16),
        values_rows.reshape(key_count, head_count, HD),
        preferred_element_type=F32,
    )
    accumulated = (
        accumulated.reshape(query_count, head_count, HD) * correction.T[:, :, None] + mixed
    )
    return (new_maxima, totals, accumulated.reshape(query_count, head_count * HD))


def attention_over(queries, pieces):
    query_count = queries.shape[0]
    head_count = queries.shape[1] // HD
    running = (
        jnp.full((head_count, query_count), -jnp.inf, F32),
        jnp.zeros((head_count, query_count), F32),
        jnp.zeros(queries.shape, F32),
    )
    for piece in pieces:
        running = attend_keys(running, queries, piece[0], piece[1])
    maxima, totals, accumulated = running
    normalized_rows = accumulated.reshape(query_count, head_count, HD) / totals.T[:, :, None]
    return normalized_rows.reshape(query_count, head_count * HD).astype(BF16)


def shifted_pieces(value, axis):
    count = lax.axis_size(axis)
    return [value] + [
        lax.ppermute(value, axis, [(i, (i + shift) % count) for i in range(count)])
        for shift in range(1, count)
    ]


def gather_columns(value, axis):
    count = lax.axis_size(axis)
    index = lax.axis_index(axis)
    width = value.shape[-1]
    whole = jnp.zeros(value.shape[:-1] + (count * width,), value.dtype)
    for shift, piece in enumerate(shifted_pieces(value, axis)):
        start = lax.rem(index - shift + count, count) * width
        whole = lax.dynamic_update_slice_in_dim(whole, piece, start, axis=value.ndim - 1)
    return whole


def sum_over(value, axis):
    total = value.astype(F32)
    for piece in shifted_pieces(value, axis)[1:]:
        total = total + piece.astype(F32)
    return total


def with_border_rows(cells):
    count = lax.axis_size("blk")
    up = [(i, i + 1) for i in range(count - 1)]
    down = [(i + 1, i) for i in range(count - 1)]
    return jnp.concatenate(
        [lax.ppermute(cells[-1:], "blk", up), cells, lax.ppermute(cells[:1], "blk", down)], axis=0
    )


def general_body(
    left_tokens, right_tokens, self_qkv, self_out, cross_qkv, cross_out, reassemble, conv_weight
):
    tiles = lax.axis_size("tile")
    tile_index = lax.axis_index("tile")
    token_count = left_tokens.shape[1]
    left_full = gather_columns(left_tokens[0], "tile")
    right_full = gather_columns(right_tokens[0], "tile")
    reassemble_full = gather_columns(reassemble.T, "tile").T
    left_normed = layer_norm(left_full)
    right_normed = layer_norm(right_full)
    self_query = project_rows(left_normed, self_qkv[0])
    self_pieces = shifted_pieces(
        jnp.stack([project_rows(left_normed, self_qkv[1]), project_rows(left_normed, self_qkv[2])]),
        "blk",
    )
    cross_pieces = shifted_pieces(
        jnp.stack(
            [project_rows(right_normed, cross_qkv[1]), project_rows(right_normed, cross_qkv[2])]
        ),
        "blk",
    )
    self_mixed = attention_over(self_query, self_pieces)
    self_term = jnp.dot(self_mixed, self_out, preferred_element_type=F32)
    self_sum = sum_over(self_term.astype(BF16), "tile")
    updated = (left_full.astype(F32) + self_sum).astype(BF16)
    cross_query = project_rows(layer_norm(updated), cross_qkv[0])
    cross_mixed = attention_over(cross_query, cross_pieces)
    cross_term = jnp.dot(cross_mixed, cross_out, preferred_element_type=F32)
    cross_sum = sum_over(cross_term.astype(BF16), "tile")
    final_tokens = (updated.astype(F32) + cross_sum).astype(BF16)
    band_rows = token_count // GRID_W
    column_count = GRID_W // tiles
    grid = jnp.pad(final_tokens.reshape(band_rows, GRID_W, -1), ((0, 0), (1, 1), (0, 0)))
    window = lax.dynamic_slice_in_dim(grid, tile_index * column_count, column_count + 2, axis=1)
    wide_map = jnp.dot(
        window.reshape(band_rows * (column_count + 2), -1),
        reassemble_full,
        preferred_element_type=F32,
    )
    wide_map = wide_map.astype(BF16).reshape(band_rows, column_count + 2, CH)
    feature_map = wide_map[:, 1 : column_count + 1]
    padded = with_border_rows(jnp.maximum(wide_map, jnp.zeros((), BF16)))
    stacked = jnp.concatenate(
        [
            padded[row_shift : row_shift + band_rows, col_shift : col_shift + column_count]
            for row_shift in range(3)
            for col_shift in range(3)
        ],
        axis=-1,
    )
    convolved = jnp.dot(
        stacked.reshape(band_rows * column_count, 9 * CH),
        conv_weight.reshape(9 * CH, CH),
        preferred_element_type=F32,
    )
    joined = feature_map.astype(F32) + convolved.reshape(band_rows, column_count, CH)
    return joined.astype(BF16)[None]


def whole_program(mesh, *arrays):
    shape = mesh.shape
    left, qkv = arrays[0], arrays[2]
    fits = (
        shape["blk"] == 4
        and shape["tile"] == 2
        and shape["pair"] == 2
        and left.shape[0] == 2 * shape["groups"]
        and left.shape[1] == 4 * ROWS
        and left.shape[2] == DIM
        and qkv.shape[2] == 2 * COLS
    )
    placed = (
        P(("groups", "pair"), "blk", "tile"),
        P(("groups", "pair"), "blk", "tile"),
        P(None, None, "tile"),
        P("tile", None),
        P(None, None, "tile"),
        P("tile", None),
        P("tile", None),
        P(),
    )
    return jax.shard_map(
        fused_body if fits else general_body,
        mesh=mesh,
        in_specs=placed,
        out_specs=P(("groups", "pair"), "blk", "tile", None),
        check_vma=False,
    )(*arrays)


def solution(mesh):
    return functools.partial(whole_program, mesh)
```

```python
import functools

import jax
import jax.numpy as jnp
from jax import lax
from jax.experimental import pallas as pl
from jax.experimental.pallas import tpu as pltpu
from jax.sharding import PartitionSpec as P

HD = 64
CH = 256
GRID_W = 128
MESH = pl.DeviceIdType.MESH
F32 = jnp.float32
BF16 = jnp.bfloat16


ROWS = 384
CHUNK = 128
NCH = ROWS // CHUNK
FEAT = 384
DIM = 2 * FEAT
COLS = 256
WIN = 80
OUTW = 64

(SW_L, X_L, SW_R, X_R, KS_Z, KS_C, KS_F, KC_Z, KC_C, KC_F, MX, PX, FM) = range(0, 39, 3)
TOP, BOT = 39, 40
SO, RA = 41, 45
N_SEMS = 49
LAST = 1

(L_WS, L_WC, L_SO, L_CO, L_RA, L_CW, L_XL, L_XR) = (0, 1, 2, 3, 4, 5, 6, 9)
N_LOCAL = 12


def normalized(a, b):
    mean = (jnp.sum(a, axis=1, keepdims=True) + jnp.sum(b, axis=1, keepdims=True)) * (1.0 / DIM)
    a, b = a - mean, b - mean
    variance = (
        jnp.sum(a * a, axis=1, keepdims=True) + jnp.sum(b * b, axis=1, keepdims=True)
    ) * (1.0 / DIM)
    scale = lax.rsqrt(variance + 1e-06)
    return jnp.concatenate([(a * scale).astype(BF16), (b * scale).astype(BF16)], axis=1)


def fused_kernel(
    lt, rt, ws_h, so_h, wc_h, co_h, ra_h, cw_h, out_ref,
    xl, xr, ws, wc, so, co, ra, cw, qd, kvs, kvc, m_s, l_s, acc_s,
    mixed, upd, w2, part, psend, precv, fms, cin, cf,
    send, recv, local,
):
    g, b, t, p = (lax.axis_index(a) for a in ("groups", "blk", "tile", "pair"))
    half = b // 2
    home = p == half
    guest = p != half
    far = 3 - b
    x_peer = (g, b, 1 - t, p)
    sibling = (g, b, t, 1 - p)
    z_peer = (g, b + 1 - 2 * lax.rem(b, 2), t, p)
    partner = (g, far, t, 1 - p)
    partner_x = (g, far, 1 - t, 1 - p)
    band = jnp.where(home, b, far)
    pair = jnp.where(home, p, 1 - p)

    def rcopy(src, dst, sem, device):
        return pltpu.make_async_remote_copy(
            src_ref=src, dst_ref=dst, send_sem=send.at[sem], recv_sem=recv.at[sem],
            device_id=device, device_id_type=MESH,
        )

    def lcopy(src, dst, sem):
        return pltpu.make_async_copy(src, dst, local.at[sem])

    def rows(c):
        return pl.ds(c * CHUNK, CHUNK)

    def own_local(arg, held, sem, c):
        return lcopy(arg.at[0, rows(c)], held.at[t, rows(c)], sem + c)

    def swap(arg, held, sem, c):
        return rcopy(arg.at[0, rows(c)], held.at[t, rows(c)], sem + c, partner)

    def across(held, sem, c):
        return rcopy(held.at[t, rows(c)], held.at[t, rows(c)], sem + c, x_peer)

    loads = [
        lcopy(ws_h, ws, L_WS),
        lcopy(wc_h, wc, L_WC),
        lcopy(so_h, so.at[t], L_SO),
        lcopy(co_h, co, L_CO),
        lcopy(ra_h, ra.at[t], L_RA),
        lcopy(cw_h, cw, L_CW),
    ]

    @pl.when(home)
    def _():
        for c in range(NCH):
            own_local(lt, xl, L_XL, c).start()

    loads[0].start()
    loads[2].start()

    @pl.when(home)
    def _():
        for c in range(NCH):
            own_local(rt, xr, L_XR, c).start()

    for k in (1, 4, 3, 5):
        loads[k].start()
    cin[...] = jnp.zeros_like(cin)
    qd[...] = jnp.zeros_like(qd)

    y_peer = (1 - g, b, t, p)

    barrier = pltpu.get_barrier_semaphore()
    for device in (y_peer, partner_x):
        pl.semaphore_signal(barrier, inc=1, device_id=device, device_id_type=MESH)
    pl.semaphore_signal(barrier, inc=1, device_id=x_peer, device_id_type=MESH)
    pl.semaphore_signal(barrier, inc=1, device_id=sibling, device_id_type=MESH)
    for k in (1, 2, 3):
        for q in range(2):
            pl.semaphore_signal(
                barrier, inc=1, device_id=(g, lax.rem(b + k, 4), t, q), device_id_type=MESH
            )
    pl.semaphore_wait(barrier, 10)

    @pl.when(guest)
    def _():
        for c in range(NCH):
            swap(lt, xl, SW_L, c).start()

    def forward_home(arg, held, l_sem, x_sem):
        @pl.when(home)
        def _():
            for c in range(NCH):
                own_local(arg, held, l_sem, c).wait()
                across(held, x_sem, c).start()

    def forward_guest(arg, held, sw_sem, x_sem, chunks):
        @pl.when(guest)
        def _():
            for c in chunks:
                swap(arg, held, sw_sem, c).wait_recv()
                across(held, x_sem, c).start()

    forward_home(lt, xl, L_XL, X_L)
    forward_guest(lt, xl, SW_L, X_L, range(NCH))

    @pl.when(guest)
    def _():
        for c in range(NCH):
            swap(rt, xr, SW_R, c).start()

    loads[0].wait()

    def chunk_normed(held, c):
        return normalized(held[0, rows(c)].astype(F32), held[1, rows(c)].astype(F32))

    def put_query(c, normed, weight):
        q = jnp.dot(normed, weight, preferred_element_type=F32).astype(BF16) * BF16(HD**-0.5)
        qt = q.T
        for hp in range(2):
            qd[c, hp, 0:HD, 0:128] = qt[128 * hp : 128 * hp + HD]
            qd[c, hp, HD:128, 128:256] = qt[128 * hp + HD : 128 * hp + 128]

    def put_keys(kv, c, normed, w_key, w_value):
        k = jnp.dot(normed, w_key, preferred_element_type=F32).astype(BF16)
        v = jnp.dot(normed, w_value, preferred_element_type=F32).astype(BF16).T
        for hp in range(2):
            kv[0, c, hp] = k[:, 128 * hp : 128 * hp + 128]
            kv[0, c, 2 + hp] = v[128 * hp : 128 * hp + 128]

    def to_z(kv, sem, c):
        return rcopy(kv.at[0, c], kv.at[2, c], sem + c, z_peer)

    def to_sibling(kv, sem, c):
        return rcopy(kv.at[0, c], kv.at[1, c], sem + c, sibling)

    def onward(kv, sem, c):
        return rcopy(kv.at[2, c], kv.at[3, c], sem + c, sibling)

    for c in range(NCH):
        across(xl, X_L, c).wait_recv()
        normed = chunk_normed(xl, c)
        put_keys(kvs, c, normed, ws[1], ws[2])
        to_z(kvs, KS_Z, c).start()
        to_sibling(kvs, KS_C, c).start()
        put_query(c, normed, ws[0])

    forward_home(rt, xr, L_XR, X_R)

    class Shared:
        def __init__(self, ref, sem):
            self.ref, self.sem, self.size = ref, sem, ref.shape[1] // 4

        def copy(self, side, quarter, k, device):
            at = pl.ds(pl.multiple_of(quarter * self.size, self.size), self.size)
            return rcopy(self.ref.at[side, at], self.ref.at[side, at], self.sem + k, device)

        def over_tile(self):
            return self.copy(t, 2 * g + p, 0, x_peer)

        def over_groups(self):
            return self.copy(1 - t, 2 * g + p, 1, y_peer)

        def to_core(self):
            return self.copy(1 - t, 2 * g + p, 2, sibling)

        def to_core_later(self):
            return self.copy(1 - t, 2 * (1 - g) + p, 3, sibling)

        def pass_on(self):
            self.over_tile().wait_recv()
            self.over_groups().start()
            self.to_core().start()

        def pass_on_later(self):
            self.over_groups().wait_recv()
            self.to_core_later().start()

        def wait_recv(self):
            self.to_core().wait_recv()
            self.to_core_later().wait_recv()

        def wait_send(self):
            self.over_tile().wait_send()
            self.over_groups().wait_send()
            self.to_core().wait_send()
            self.to_core_later().wait_send()

    so_copy, ra_copy = Shared(so, SO), Shared(ra, RA)
    loads[2].wait()
    so_copy.over_tile().start()
    loads[4].wait()
    ra_copy.over_tile().start()
    loads[1].wait()

    def flash(kv, slots, chunks, first):
        units = [(c, hp) for c in chunks for hp in range(2)]
        keys = [[kv[slot, :, hp].reshape(ROWS, 128) for slot in slots] for hp in range(2)]
        values = [
            [
                jnp.concatenate([kv[slot, i, 2 + hp] for i in range(NCH)], axis=1)
                for slot in slots
            ]
            for hp in range(2)
        ]
        scores = [
            [jnp.dot(k, qd[c, hp], preferred_element_type=F32) for k in keys[hp]]
            for c, hp in units
        ]
        if not first:
            held = [(m_s[2 * c + hp], l_s[2 * c + hp], acc_s[2 * c + hp]) for c, hp in units]
        results = []
        for i, (c, hp) in enumerate(units):
            tops = [jnp.max(block, axis=0, keepdims=True) for block in scores[i]]
            top = functools.reduce(jnp.maximum, tops)
            if not first:
                top = jnp.maximum(held[i][0], top)
            total, pv = 0.0, 0.0
            for block, value in zip(scores[i], values[hp]):
                e = jnp.exp(block - top)
                total = total + jnp.sum(e, axis=0, keepdims=True)
                pv = pv + jnp.dot(value, e.astype(BF16), preferred_element_type=F32)
            upper, lower = pv[0:HD, 0:128], pv[HD:128, 128:256]
            if not first:
                fix = jnp.exp(held[i][0] - top)
                total = total + held[i][1] * fix
                upper = upper + held[i][2][0:HD] * fix[:, 0:128]
                lower = lower + held[i][2][HD:128] * fix[:, 128:256]
            results.append((top, total, upper, lower))
        for i, (c, hp) in enumerate(units):
            u = c * 2 + hp
            m_s[u], l_s[u], acc_s[u, 0:HD], acc_s[u, HD:128] = results[i]

    def slot_of(step):
        return jnp.where(home, (0, 2, 1, 3)[step], (0, 1, 3, 2)[step])

    def from_z(kv, z_sem, f_sem):
        for c in range(NCH):
            to_z(kv, z_sem, c).wait_recv()
            onward(kv, f_sem, c).start()

    def arrive(kv, step, z_sem, c_sem, f_sem):
        @pl.when(home)
        def _():
            if step == 1:
                from_z(kv, z_sem, f_sem)
            for c in range(NCH):
                if step == 2:
                    to_sibling(kv, c_sem, c).wait_recv()
                if step == 3:
                    onward(kv, f_sem, c).wait_recv()

        @pl.when(guest)
        def _():
            if step == 3:
                from_z(kv, z_sem, f_sem)
            for c in range(NCH):
                if step == 1:
                    to_sibling(kv, c_sem, c).wait_recv()
                if step == 2:
                    onward(kv, f_sem, c).wait_recv()

    def finished(c):
        parts = []
        for hp in range(2):
            u = c * 2 + hp
            total = l_s[u]
            o = jnp.concatenate(
                [acc_s[u, 0:HD] / total[:, 0:128], acc_s[u, HD:128] / total[:, 128:256]], axis=0
            )
            parts.append(o.T.astype(BF16))
        return jnp.concatenate(parts, axis=1)

    every = range(NCH)
    self_sems, cross_sems = (KS_Z, KS_C, KS_F), (KC_Z, KC_C, KC_F)
    def right_keys():
        for c in range(NCH):
            across(xr, X_R, c).wait_recv()
            normed = chunk_normed(xr, c)
            put_keys(kvc, c, normed, wc[1], wc[2])
            to_z(kvc, KC_Z, c).start()
            to_sibling(kvc, KC_C, c).start()

    flash(kvs, [0], every, True)
    forward_guest(rt, xr, SW_R, X_R, [0])
    arrive(kvs, 1, *self_sems)
    flash(kvs, [slot_of(1)], every, False)
    forward_guest(rt, xr, SW_R, X_R, [1])

    arrive(kvs, 2, *self_sems)
    flash(kvs, [slot_of(2)], every, False)
    forward_guest(rt, xr, SW_R, X_R, [2])
    @pl.when(home)
    def _():
        right_keys()

    so_copy.pass_on()
    ra_copy.pass_on()
    arrive(kvs, 3, *self_sems)


    def mixed_across(c):
        return rcopy(mixed.at[t, rows(c)], mixed.at[t, rows(c)], MX + c, x_peer)

    for c in range(NCH):
        flash(kvs, [slot_of(3)], [c], False)
        mixed[t, rows(c)] = finished(c)
        mixed_across(c).start()

    @pl.when(guest)
    def _():
        right_keys()

    so_copy.pass_on_later()
    ra_copy.pass_on_later()
    so_copy.wait_recv()
    for c in range(NCH):
        mixed_across(c).wait_recv()
        both = jnp.concatenate([mixed[0, rows(c)], mixed[1, rows(c)]], axis=1)
        term = jnp.dot(both, so[...].reshape(2 * COLS, DIM), preferred_element_type=F32)
        a = (xl[0, rows(c)].astype(F32) + term[:, :FEAT]).astype(BF16)
        d = (xl[1, rows(c)].astype(F32) + term[:, FEAT:]).astype(BF16)
        upd[rows(c), 0:FEAT] = a
        upd[rows(c), FEAT:DIM] = d
        put_query(c, normalized(a.astype(F32), d.astype(F32)), wc[0])

    flash(kvc, [0], every, True)
    arrive(kvc, 1, *cross_sems)
    flash(kvc, [slot_of(1)], every, False)
    loads[3].wait()
    ra_copy.wait_recv()
    w2[...] = jnp.dot(co[...], ra[...].reshape(DIM, CH), preferred_element_type=F32).astype(BF16)
    arrive(kvc, 2, *cross_sems)
    arrive(kvc, 3, *cross_sems)

    def partial_across(c):
        return rcopy(psend.at[c], precv.at[c], PX + c, x_peer)

    def partial_home(c):
        return rcopy(psend.at[c], precv.at[c], PX + c, partner_x)

    place = pl.ds(pl.multiple_of(16 * (1 - t), 16), WIN)

    def map_home(c):
        return rcopy(fms.at[c], cin.at[1 + c, place], FM + c, partner)

    def map_above():
        return rcopy(fms.at[0], cin.at[4, place], TOP, (g, band - 1, t, pair))

    def map_below():
        return rcopy(fms.at[NCH - 1], cin.at[0, place], BOT, (g, band + 1, t, pair))

    mine = pl.ds(pl.multiple_of(48 * t, 16), WIN)
    theirs = pl.ds(pl.multiple_of(48 * (1 - t), 16), WIN)

    def send_partial(c):
        flash(kvc, [slot_of(2), slot_of(3)], [c], False)
        part[c] = jnp.dot(finished(c), w2[...], preferred_element_type=F32)
        psend[c] = part[c, theirs].astype(BF16)
        if c != LAST:
            partial_across(c).start()
            return

        @pl.when(home)
        def _():
            partial_across(c).start()

        @pl.when(guest)
        def _():
            partial_home(c).start()

    def own_map(c):
        tokens = upd[pl.ds(pl.multiple_of(c * CHUNK + 48 * t, 16), WIN)]
        base = jnp.dot(tokens, ra[...].reshape(DIM, CH), preferred_element_type=F32)
        return base + part[c, mine]

    def send_map(c):
        row = own_map(c)
        partial_across(c).wait_recv()
        row = (row + precv[c].astype(F32)).astype(BF16)
        fms[c] = row

        @pl.when(guest)
        def _():
            map_home(c).start()

        @pl.when(home)
        def _():
            cin[1 + c, place] = row

        if c == 0:

            @pl.when(band > 0)
            def _():
                map_above().start()

        if c == NCH - 1:

            @pl.when(band < 3)
            def _():
                map_below().start()

    def send_last():
        row = own_map(LAST)

        @pl.when(guest)
        def _():
            fms[LAST] = row.astype(BF16)
            map_home(LAST).start()
            map_home(LAST).wait_recv()
            partial_home(LAST).wait_recv()
            cin[1 + LAST, place] = (
                cin[1 + LAST, place].astype(F32) + precv[LAST].astype(F32)
            ).astype(BF16)

        @pl.when(home)
        def _():
            partial_across(LAST).wait_recv()
            cin[1 + LAST, place] = (row + precv[LAST].astype(F32)).astype(BF16)

    send_partial(0)
    send_partial(2)
    send_map(0)
    send_partial(1)
    send_map(2)
    send_last()

    loads[5].wait()

    @pl.when(guest)
    def _():
        for c in (0, NCH - 1):
            map_home(c).wait_recv()

    @pl.when(b < 3)
    def _():
        map_above().wait_recv()

    @pl.when(b > 0)
    def _():
        map_below().wait_recv()

    cf[...] = jnp.maximum(cin[...].astype(F32), 0.0)
    shifted = jnp.concatenate(
        [
            cf[:, 15 + s : 15 + s + OUTW].astype(BF16).reshape((NCH + 2) * OUTW, CH)
            for s in range(3)
        ],
        axis=1,
    )
    total = cin[1 : 1 + NCH, 16 : 16 + OUTW].astype(F32).reshape(NCH * OUTW, CH)
    for a in range(3):
        total = total + jnp.dot(
            shifted[a * OUTW : (a + NCH) * OUTW],
            cw[a].reshape(3 * CH, CH),
            preferred_element_type=F32,
        )
    out_ref[0] = total.astype(BF16).reshape(NCH, OUTW, CH)

    @pl.when(guest)
    def _():
        for c in range(NCH):
            swap(lt, xl, SW_L, c).wait_send()
            swap(rt, xr, SW_R, c).wait_send()
            map_home(c).wait_send()
        partial_home(LAST).wait_send()

    for c in range(NCH):
        across(xl, X_L, c).wait_send()
        across(xr, X_R, c).wait_send()
        for kv, z_sem, c_sem, f_sem in ((kvs, KS_Z, KS_C, KS_F), (kvc, KC_Z, KC_C, KC_F)):
            to_z(kv, z_sem, c).wait_send()
            to_sibling(kv, c_sem, c).wait_send()
            onward(kv, f_sem, c).wait_send()
        mixed_across(c).wait_send()
        if c != LAST:
            partial_across(c).wait_send()
    so_copy.wait_send()
    ra_copy.wait_send()

    @pl.when(home)
    def _():
        partial_across(LAST).wait_send()

    @pl.when(band > 0)
    def _():
        map_above().wait_send()

    @pl.when(band < 3)
    def _():
        map_below().wait_send()


def fused_body(*arrays):
    hbm = pl.BlockSpec(memory_space=pl.ANY)
    return pl.pallas_call(
        fused_kernel,
        out_shape=jax.ShapeDtypeStruct((1, NCH, OUTW, CH), BF16),
        in_specs=[hbm] * len(arrays),
        out_specs=pl.BlockSpec(memory_space=pltpu.VMEM),
        scratch_shapes=[
            pltpu.VMEM((2, ROWS, FEAT), BF16),
            pltpu.VMEM((2, ROWS, FEAT), BF16),
            pltpu.VMEM((3, DIM, COLS), BF16),
            pltpu.VMEM((3, DIM, COLS), BF16),
            pltpu.VMEM((2, COLS, DIM), BF16),
            pltpu.VMEM((COLS, DIM), BF16),
            pltpu.VMEM((2, FEAT, CH), BF16),
            pltpu.VMEM((3, 3, CH, CH), BF16),
            pltpu.VMEM((NCH, 2, 128, 256), BF16),
            pltpu.VMEM((4, NCH, 4, 128, 128), BF16),
            pltpu.VMEM((4, NCH, 4, 128, 128), BF16),
            pltpu.VMEM((2 * NCH, 1, 256), F32),
            pltpu.VMEM((2 * NCH, 1, 256), F32),
            pltpu.VMEM((2 * NCH, 128, 128), F32),
            pltpu.VMEM((2, ROWS, COLS), BF16),
            pltpu.VMEM((ROWS, DIM), BF16),
            pltpu.VMEM((COLS, CH), BF16),
            pltpu.VMEM((NCH, CHUNK, CH), F32),
            pltpu.VMEM((NCH, WIN, CH), BF16),
            pltpu.VMEM((NCH, WIN, CH), BF16),
            pltpu.VMEM((NCH, WIN, CH), BF16),
            pltpu.VMEM((NCH + 2, 96, CH), BF16),
            pltpu.VMEM((NCH + 2, 96, CH), F32),
            pltpu.SemaphoreType.DMA((N_SEMS,)),
            pltpu.SemaphoreType.DMA((N_SEMS,)),
            pltpu.SemaphoreType.DMA((N_LOCAL,)),
        ],
        compiler_params=pltpu.CompilerParams(
            collective_id=0, has_side_effects=True, vmem_limit_bytes=56 * 2**20
        ),
        cost_estimate=pl.CostEstimate(
            flops=3 * 10**9, bytes_accessed=6 * 10**6, transcendentals=5 * 10**6
        ),
        name="decoder",
    )(*arrays)


def layer_norm(values):
    widened = values.astype(F32)
    centred = widened - jnp.mean(widened, axis=-1, keepdims=True)
    variance = jnp.mean(centred * centred, axis=-1, keepdims=True)
    return (centred * lax.rsqrt(variance + 1e-06)).astype(BF16)


def project_rows(normed, weight):
    return jnp.dot(normed, weight, preferred_element_type=F32).astype(BF16)


def attend_keys(running, queries, keys_rows, values_rows):
    maxima, totals, accumulated = running
    query_count = queries.shape[0]
    head_count = queries.shape[1] // HD
    key_count = keys_rows.shape[0]
    scores = jnp.einsum(
        "qhd,khd->hqk",
        queries.reshape(query_count, head_count, HD),
        keys_rows.reshape(key_count, head_count, HD),
        preferred_element_type=F32,
    ) * HD ** (-0.5)
    new_maxima = jnp.maximum(maxima, jnp.max(scores, axis=2))
    correction = jnp.exp(maxima - new_maxima)
    expanded = jnp.exp(scores - new_maxima[:, :, None])
    totals = totals * correction + jnp.sum(expanded, axis=2)
    mixed = jnp.einsum(
        "hqk,khd->qhd",
        expanded.astype(BF16),
        values_rows.reshape(key_count, head_count, HD),
        preferred_element_type=F32,
    )
    accumulated = (
        accumulated.reshape(query_count, head_count, HD) * correction.T[:, :, None] + mixed
    )
    return (new_maxima, totals, accumulated.reshape(query_count, head_count * HD))


def attention_over(queries, pieces):
    query_count = queries.shape[0]
    head_count = queries.shape[1] // HD
    running = (
        jnp.full((head_count, query_count), -jnp.inf, F32),
        jnp.zeros((head_count, query_count), F32),
        jnp.zeros(queries.shape, F32),
    )
    for piece in pieces:
        running = attend_keys(running, queries, piece[0], piece[1])
    maxima, totals, accumulated = running
    normalized_rows = accumulated.reshape(query_count, head_count, HD) / totals.T[:, :, None]
    return normalized_rows.reshape(query_count, head_count * HD).astype(BF16)


def shifted_pieces(value, axis):
    count = lax.axis_size(axis)
    return [value] + [
        lax.ppermute(value, axis, [(i, (i + shift) % count) for i in range(count)])
        for shift in range(1, count)
    ]


def gather_columns(value, axis):
    count = lax.axis_size(axis)
    index = lax.axis_index(axis)
    width = value.shape[-1]
    whole = jnp.zeros(value.shape[:-1] + (count * width,), value.dtype)
    for shift, piece in enumerate(shifted_pieces(value, axis)):
        start = lax.rem(index - shift + count, count) * width
        whole = lax.dynamic_update_slice_in_dim(whole, piece, start, axis=value.ndim - 1)
    return whole


def sum_over(value, axis):
    total = value.astype(F32)
    for piece in shifted_pieces(value, axis)[1:]:
        total = total + piece.astype(F32)
    return total


def with_border_rows(cells):
    count = lax.axis_size("blk")
    up = [(i, i + 1) for i in range(count - 1)]
    down = [(i + 1, i) for i in range(count - 1)]
    return jnp.concatenate(
        [lax.ppermute(cells[-1:], "blk", up), cells, lax.ppermute(cells[:1], "blk", down)], axis=0
    )


def general_body(
    left_tokens, right_tokens, self_qkv, self_out, cross_qkv, cross_out, reassemble, conv_weight
):
    tiles = lax.axis_size("tile")
    tile_index = lax.axis_index("tile")
    token_count = left_tokens.shape[1]
    left_full = gather_columns(left_tokens[0], "tile")
    right_full = gather_columns(right_tokens[0], "tile")
    reassemble_full = gather_columns(reassemble.T, "tile").T
    left_normed = layer_norm(left_full)
    right_normed = layer_norm(right_full)
    self_query = project_rows(left_normed, self_qkv[0])
    self_pieces = shifted_pieces(
        jnp.stack([project_rows(left_normed, self_qkv[1]), project_rows(left_normed, self_qkv[2])]),
        "blk",
    )
    cross_pieces = shifted_pieces(
        jnp.stack(
            [project_rows(right_normed, cross_qkv[1]), project_rows(right_normed, cross_qkv[2])]
        ),
        "blk",
    )
    self_mixed = attention_over(self_query, self_pieces)
    self_term = jnp.dot(self_mixed, self_out, preferred_element_type=F32)
    self_sum = sum_over(self_term.astype(BF16), "tile")
    updated = (left_full.astype(F32) + self_sum).astype(BF16)
    cross_query = project_rows(layer_norm(updated), cross_qkv[0])
    cross_mixed = attention_over(cross_query, cross_pieces)
    cross_term = jnp.dot(cross_mixed, cross_out, preferred_element_type=F32)
    cross_sum = sum_over(cross_term.astype(BF16), "tile")
    final_tokens = (updated.astype(F32) + cross_sum).astype(BF16)
    band_rows = token_count // GRID_W
    column_count = GRID_W // tiles
    grid = jnp.pad(final_tokens.reshape(band_rows, GRID_W, -1), ((0, 0), (1, 1), (0, 0)))
    window = lax.dynamic_slice_in_dim(grid, tile_index * column_count, column_count + 2, axis=1)
    wide_map = jnp.dot(
        window.reshape(band_rows * (column_count + 2), -1),
        reassemble_full,
        preferred_element_type=F32,
    )
    wide_map = wide_map.astype(BF16).reshape(band_rows, column_count + 2, CH)
    feature_map = wide_map[:, 1 : column_count + 1]
    padded = with_border_rows(jnp.maximum(wide_map, jnp.zeros((), BF16)))
    stacked = jnp.concatenate(
        [
            padded[row_shift : row_shift + band_rows, col_shift : col_shift + column_count]
            for row_shift in range(3)
            for col_shift in range(3)
        ],
        axis=-1,
    )
    convolved = jnp.dot(
        stacked.reshape(band_rows * column_count, 9 * CH),
        conv_weight.reshape(9 * CH, CH),
        preferred_element_type=F32,
    )
    joined = feature_map.astype(F32) + convolved.reshape(band_rows, column_count, CH)
    return joined.astype(BF16)[None]


def whole_program(mesh, *arrays):
    shape = mesh.shape
    left, qkv = arrays[0], arrays[2]
    fits = (
        shape["blk"] == 4
        and shape["tile"] == 2
        and shape["pair"] == 2
        and left.shape[0] == 2 * shape["groups"]
        and left.shape[1] == 4 * ROWS
        and left.shape[2] == DIM
        and qkv.shape[2] == 2 * COLS
    )
    placed = (
        P(("groups", "pair"), "blk", "tile"),
        P(("groups", "pair"), "blk", "tile"),
        P(None, None, "tile"),
        P("tile", None),
        P(None, None, "tile"),
        P("tile", None),
        P("tile", None),
        P(),
    )
    return jax.shard_map(
        fused_body if fits else general_body,
        mesh=mesh,
        in_specs=placed,
        out_specs=P(("groups", "pair"), "blk", "tile", None),
        check_vma=False,
    )(*arrays)


def solution(mesh):
    return functools.partial(whole_program, mesh)
```

```python
import functools

import jax
import jax.numpy as jnp
from jax import lax
from jax.experimental import pallas as pl
from jax.experimental.pallas import tpu as pltpu
from jax.sharding import PartitionSpec as P

HD = 64
CH = 256
GRID_W = 128
MESH = pl.DeviceIdType.MESH
F32 = jnp.float32
BF16 = jnp.bfloat16


ROWS = 384
CHUNK = 128
NCH = ROWS // CHUNK
FEAT = 384
DIM = 2 * FEAT
COLS = 256
WIN = 80
OUTW = 64

(SW_L, X_L, SW_R, X_R, KS_Z, KS_C, KS_F, KC_Z, KC_C, KC_F, MX, PX, FM) = range(0, 39, 3)
TOP, BOT = 39, 40
SO, RA = 41, 45
N_SEMS = 49
LAST = 1

(L_WS, L_WC, L_SO, L_CO, L_RA, L_CW, L_XL, L_XR) = (0, 1, 2, 3, 4, 5, 6, 9)
N_LOCAL = 12


def normalized(a, b):
    mean = (jnp.sum(a, axis=1, keepdims=True) + jnp.sum(b, axis=1, keepdims=True)) * (1.0 / DIM)
    a, b = a - mean, b - mean
    variance = (
        jnp.sum(a * a, axis=1, keepdims=True) + jnp.sum(b * b, axis=1, keepdims=True)
    ) * (1.0 / DIM)
    scale = lax.rsqrt(variance + 1e-06)
    return jnp.concatenate([(a * scale).astype(BF16), (b * scale).astype(BF16)], axis=1)


def fused_kernel(
    lt, rt, ws_h, so_h, wc_h, co_h, ra_h, cw_h, out_ref,
    xl, xr, ws, wc, so, co, ra, cw, qd, kvs, kvc, m_s, l_s, acc_s,
    mixed, upd, w2, part, base, psend, precv, fms, cin, cf,
    send, recv, local,
):
    g, b, t, p = (lax.axis_index(a) for a in ("groups", "blk", "tile", "pair"))
    half = b // 2
    home = p == half
    guest = p != half
    far = 3 - b
    x_peer = (g, b, 1 - t, p)
    sibling = (g, b, t, 1 - p)
    z_peer = (g, b + 1 - 2 * lax.rem(b, 2), t, p)
    partner = (g, far, t, 1 - p)
    partner_x = (g, far, 1 - t, 1 - p)
    band = jnp.where(home, b, far)
    pair = jnp.where(home, p, 1 - p)

    def rcopy(src, dst, sem, device):
        return pltpu.make_async_remote_copy(
            src_ref=src, dst_ref=dst, send_sem=send.at[sem], recv_sem=recv.at[sem],
            device_id=device, device_id_type=MESH,
        )

    def lcopy(src, dst, sem):
        return pltpu.make_async_copy(src, dst, local.at[sem])

    def rows(c):
        return pl.ds(c * CHUNK, CHUNK)

    def own_local(arg, held, sem, c):
        return lcopy(arg.at[0, rows(c)], held.at[t, rows(c)], sem + c)

    def swap(arg, held, sem, c):
        return rcopy(arg.at[0, rows(c)], held.at[t, rows(c)], sem + c, partner)

    def across(held, sem, c):
        return rcopy(held.at[t, rows(c)], held.at[t, rows(c)], sem + c, x_peer)

    loads = [
        lcopy(ws_h, ws, L_WS),
        lcopy(wc_h, wc, L_WC),
        lcopy(so_h, so.at[t], L_SO),
        lcopy(co_h, co, L_CO),
        lcopy(ra_h, ra.at[t], L_RA),
        lcopy(cw_h, cw, L_CW),
    ]

    @pl.when(home)
    def _():
        for c in range(NCH):
            own_local(lt, xl, L_XL, c).start()

    loads[0].start()
    loads[2].start()

    @pl.when(home)
    def _():
        for c in range(NCH):
            own_local(rt, xr, L_XR, c).start()

    for k in (1, 4, 3, 5):
        loads[k].start()
    cin[...] = jnp.zeros_like(cin)
    qd[...] = jnp.zeros_like(qd)

    y_peer = (1 - g, b, t, p)

    barrier = pltpu.get_barrier_semaphore()
    for device in (y_peer, partner_x):
        pl.semaphore_signal(barrier, inc=1, device_id=device, device_id_type=MESH)
    pl.semaphore_signal(barrier, inc=1, device_id=x_peer, device_id_type=MESH)
    pl.semaphore_signal(barrier, inc=1, device_id=sibling, device_id_type=MESH)
    for k in (1, 2, 3):
        for q in range(2):
            pl.semaphore_signal(
                barrier, inc=1, device_id=(g, lax.rem(b + k, 4), t, q), device_id_type=MESH
            )
    pl.semaphore_wait(barrier, 10)

    @pl.when(guest)
    def _():
        for c in range(NCH):
            swap(lt, xl, SW_L, c).start()

    def forward_home(arg, held, l_sem, x_sem):
        @pl.when(home)
        def _():
            for c in range(NCH):
                own_local(arg, held, l_sem, c).wait()
                across(held, x_sem, c).start()

    def forward_guest(arg, held, sw_sem, x_sem, chunks):
        @pl.when(guest)
        def _():
            for c in chunks:
                swap(arg, held, sw_sem, c).wait_recv()
                across(held, x_sem, c).start()

    forward_home(lt, xl, L_XL, X_L)
    forward_guest(lt, xl, SW_L, X_L, range(NCH))

    @pl.when(guest)
    def _():
        for c in range(NCH):
            swap(rt, xr, SW_R, c).start()

    loads[0].wait()

    def chunk_normed(held, c):
        return normalized(held[0, rows(c)].astype(F32), held[1, rows(c)].astype(F32))

    def put_query(c, normed, weight):
        q = jnp.dot(normed, weight, preferred_element_type=F32).astype(BF16) * BF16(HD**-0.5)
        qt = q.T
        for hp in range(2):
            qd[c, hp, 0:HD, 0:128] = qt[128 * hp : 128 * hp + HD]
            qd[c, hp, HD:128, 128:256] = qt[128 * hp + HD : 128 * hp + 128]

    def put_keys(kv, c, normed, w_key, w_value):
        k = jnp.dot(normed, w_key, preferred_element_type=F32).astype(BF16)
        v = jnp.dot(normed, w_value, preferred_element_type=F32).astype(BF16).T
        for hp in range(2):
            kv[0, c, hp] = k[:, 128 * hp : 128 * hp + 128]
            kv[0, c, 2 + hp] = v[128 * hp : 128 * hp + 128]

    def to_z(kv, sem, c):
        return rcopy(kv.at[0, c], kv.at[2, c], sem + c, z_peer)

    def to_sibling(kv, sem, c):
        return rcopy(kv.at[0, c], kv.at[1, c], sem + c, sibling)

    def onward(kv, sem, c):
        return rcopy(kv.at[2, c], kv.at[3, c], sem + c, sibling)

    for c in range(NCH):
        across(xl, X_L, c).wait_recv()
        normed = chunk_normed(xl, c)
        put_keys(kvs, c, normed, ws[1], ws[2])
        to_z(kvs, KS_Z, c).start()
        to_sibling(kvs, KS_C, c).start()
        put_query(c, normed, ws[0])

    forward_home(rt, xr, L_XR, X_R)

    class Shared:
        def __init__(self, ref, sem):
            self.ref, self.sem, self.size = ref, sem, ref.shape[1] // 4

        def copy(self, side, quarter, k, device):
            at = pl.ds(pl.multiple_of(quarter * self.size, self.size), self.size)
            return rcopy(self.ref.at[side, at], self.ref.at[side, at], self.sem + k, device)

        def over_tile(self):
            return self.copy(t, 2 * g + p, 0, x_peer)

        def over_groups(self):
            return self.copy(1 - t, 2 * g + p, 1, y_peer)

        def to_core(self):
            return self.copy(1 - t, 2 * g + p, 2, sibling)

        def to_core_later(self):
            return self.copy(1 - t, 2 * (1 - g) + p, 3, sibling)

        def pass_on(self):
            self.over_tile().wait_recv()
            self.over_groups().start()
            self.to_core().start()

        def pass_on_later(self):
            self.over_groups().wait_recv()
            self.to_core_later().start()

        def wait_recv(self):
            self.to_core().wait_recv()
            self.to_core_later().wait_recv()

        def wait_send(self):
            self.over_tile().wait_send()
            self.over_groups().wait_send()
            self.to_core().wait_send()
            self.to_core_later().wait_send()

    so_copy, ra_copy = Shared(so, SO), Shared(ra, RA)
    loads[2].wait()
    so_copy.over_tile().start()
    loads[4].wait()
    ra_copy.over_tile().start()
    loads[1].wait()

    def flash(kv, slots, chunks, first):
        units = [(c, hp) for c in chunks for hp in range(2)]
        keys = [[kv[slot, :, hp].reshape(ROWS, 128) for slot in slots] for hp in range(2)]
        values = [
            [
                jnp.concatenate([kv[slot, i, 2 + hp] for i in range(NCH)], axis=1)
                for slot in slots
            ]
            for hp in range(2)
        ]
        scores = [
            [jnp.dot(k, qd[c, hp], preferred_element_type=F32) for k in keys[hp]]
            for c, hp in units
        ]
        if not first:
            held = [(m_s[2 * c + hp], l_s[2 * c + hp], acc_s[2 * c + hp]) for c, hp in units]
        results = []
        for i, (c, hp) in enumerate(units):
            tops = [jnp.max(block, axis=0, keepdims=True) for block in scores[i]]
            top = functools.reduce(jnp.maximum, tops)
            if not first:
                top = jnp.maximum(held[i][0], top)
            total, pv = 0.0, 0.0
            for block, value in zip(scores[i], values[hp]):
                e = jnp.exp(block - top)
                total = total + jnp.sum(e, axis=0, keepdims=True)
                pv = pv + jnp.dot(value, e.astype(BF16), preferred_element_type=F32)
            upper, lower = pv[0:HD, 0:128], pv[HD:128, 128:256]
            if not first:
                fix = jnp.exp(held[i][0] - top)
                total = total + held[i][1] * fix
                upper = upper + held[i][2][0:HD] * fix[:, 0:128]
                lower = lower + held[i][2][HD:128] * fix[:, 128:256]
            results.append((top, total, upper, lower))
        for i, (c, hp) in enumerate(units):
            u = c * 2 + hp
            m_s[u], l_s[u], acc_s[u, 0:HD], acc_s[u, HD:128] = results[i]

    def slot_of(step):
        return jnp.where(home, (0, 2, 1, 3)[step], (0, 1, 3, 2)[step])

    def from_z(kv, z_sem, f_sem):
        for c in range(NCH):
            to_z(kv, z_sem, c).wait_recv()
            onward(kv, f_sem, c).start()

    def arrive(kv, step, z_sem, c_sem, f_sem):
        @pl.when(home)
        def _():
            if step == 1:
                from_z(kv, z_sem, f_sem)
            for c in range(NCH):
                if step == 2:
                    to_sibling(kv, c_sem, c).wait_recv()
                if step == 3:
                    onward(kv, f_sem, c).wait_recv()

        @pl.when(guest)
        def _():
            if step == 3:
                from_z(kv, z_sem, f_sem)
            for c in range(NCH):
                if step == 1:
                    to_sibling(kv, c_sem, c).wait_recv()
                if step == 2:
                    onward(kv, f_sem, c).wait_recv()

    def finished(c):
        parts = []
        for hp in range(2):
            u = c * 2 + hp
            total = l_s[u]
            o = jnp.concatenate(
                [acc_s[u, 0:HD] / total[:, 0:128], acc_s[u, HD:128] / total[:, 128:256]], axis=0
            )
            parts.append(o.T.astype(BF16))
        return jnp.concatenate(parts, axis=1)

    every = range(NCH)
    self_sems, cross_sems = (KS_Z, KS_C, KS_F), (KC_Z, KC_C, KC_F)
    def right_keys():
        for c in range(NCH):
            across(xr, X_R, c).wait_recv()
            normed = chunk_normed(xr, c)
            put_keys(kvc, c, normed, wc[1], wc[2])
            to_z(kvc, KC_Z, c).start()
            to_sibling(kvc, KC_C, c).start()

    flash(kvs, [0], every, True)
    forward_guest(rt, xr, SW_R, X_R, [0])
    arrive(kvs, 1, *self_sems)
    flash(kvs, [slot_of(1)], every, False)
    forward_guest(rt, xr, SW_R, X_R, [1])

    arrive(kvs, 2, *self_sems)
    flash(kvs, [slot_of(2)], every, False)
    forward_guest(rt, xr, SW_R, X_R, [2])
    @pl.when(home)
    def _():
        right_keys()

    so_copy.pass_on()
    ra_copy.pass_on()
    arrive(kvs, 3, *self_sems)


    def mixed_across(c):
        return rcopy(mixed.at[t, rows(c)], mixed.at[t, rows(c)], MX + c, x_peer)

    for c in range(NCH):
        flash(kvs, [slot_of(3)], [c], False)
        mixed[t, rows(c)] = finished(c)
        mixed_across(c).start()

    @pl.when(guest)
    def _():
        right_keys()

    so_copy.pass_on_later()
    ra_copy.pass_on_later()
    so_copy.wait_recv()
    for c in range(NCH):
        mixed_across(c).wait_recv()
        both = jnp.concatenate([mixed[0, rows(c)], mixed[1, rows(c)]], axis=1)
        term = jnp.dot(both, so[...].reshape(2 * COLS, DIM), preferred_element_type=F32)
        a = (xl[0, rows(c)].astype(F32) + term[:, :FEAT]).astype(BF16)
        d = (xl[1, rows(c)].astype(F32) + term[:, FEAT:]).astype(BF16)
        upd[rows(c), 0:FEAT] = a
        upd[rows(c), FEAT:DIM] = d
        put_query(c, normalized(a.astype(F32), d.astype(F32)), wc[0])

    flash(kvc, [0], every, True)
    arrive(kvc, 1, *cross_sems)
    flash(kvc, [slot_of(1)], every, False)
    loads[3].wait()
    ra_copy.wait_recv()
    w2[...] = jnp.dot(co[...], ra[...].reshape(DIM, CH), preferred_element_type=F32).astype(BF16)
    for c in range(NCH):
        tokens = upd[pl.ds(pl.multiple_of(c * CHUNK + 48 * t, 16), WIN)]
        base[c] = jnp.dot(tokens, ra[...].reshape(DIM, CH), preferred_element_type=F32)
    arrive(kvc, 2, *cross_sems)
    arrive(kvc, 3, *cross_sems)

    def partial_across(c):
        return rcopy(psend.at[c], precv.at[c], PX + c, x_peer)

    def partial_home(c):
        return rcopy(psend.at[c], precv.at[c], PX + c, partner_x)

    place = pl.ds(pl.multiple_of(16 * (1 - t), 16), WIN)

    def map_home(c):
        return rcopy(fms.at[c], cin.at[1 + c, place], FM + c, partner)

    def map_above():
        return rcopy(fms.at[0], cin.at[4, place], TOP, (g, band - 1, t, pair))

    def map_below():
        return rcopy(fms.at[NCH - 1], cin.at[0, place], BOT, (g, band + 1, t, pair))

    mine = pl.ds(pl.multiple_of(48 * t, 16), WIN)
    theirs = pl.ds(pl.multiple_of(48 * (1 - t), 16), WIN)

    def send_partial(c):
        flash(kvc, [slot_of(2), slot_of(3)], [c], False)
        part[c] = jnp.dot(finished(c), w2[...], preferred_element_type=F32)
        psend[c] = part[c, theirs].astype(BF16)
        if c != LAST:
            partial_across(c).start()
            return

        @pl.when(home)
        def _():
            partial_across(c).start()

        @pl.when(guest)
        def _():
            partial_home(c).start()

    def own_map(c):
        return base[c] + part[c, mine]

    def send_map(c):
        row = own_map(c)
        partial_across(c).wait_recv()
        row = (row + precv[c].astype(F32)).astype(BF16)
        fms[c] = row

        @pl.when(guest)
        def _():
            map_home(c).start()

        @pl.when(home)
        def _():
            cin[1 + c, place] = row

        if c == 0:

            @pl.when(band > 0)
            def _():
                map_above().start()

        if c == NCH - 1:

            @pl.when(band < 3)
            def _():
                map_below().start()

    def send_last():
        row = own_map(LAST)

        @pl.when(guest)
        def _():
            fms[LAST] = row.astype(BF16)
            map_home(LAST).start()
            map_home(LAST).wait_recv()
            partial_home(LAST).wait_recv()
            cin[1 + LAST, place] = (
                cin[1 + LAST, place].astype(F32) + precv[LAST].astype(F32)
            ).astype(BF16)

        @pl.when(home)
        def _():
            partial_across(LAST).wait_recv()
            cin[1 + LAST, place] = (row + precv[LAST].astype(F32)).astype(BF16)

    send_partial(0)
    send_partial(2)
    send_map(0)
    send_partial(1)
    send_map(2)
    send_last()

    loads[5].wait()

    @pl.when(guest)
    def _():
        for c in (0, NCH - 1):
            map_home(c).wait_recv()

    @pl.when(b < 3)
    def _():
        map_above().wait_recv()

    @pl.when(b > 0)
    def _():
        map_below().wait_recv()

    cf[...] = jnp.maximum(cin[...].astype(F32), 0.0)
    shifted = jnp.concatenate(
        [
            cf[:, 15 + s : 15 + s + OUTW].astype(BF16).reshape((NCH + 2) * OUTW, CH)
            for s in range(3)
        ],
        axis=1,
    )
    total = cin[1 : 1 + NCH, 16 : 16 + OUTW].astype(F32).reshape(NCH * OUTW, CH)
    for a in range(3):
        total = total + jnp.dot(
            shifted[a * OUTW : (a + NCH) * OUTW],
            cw[a].reshape(3 * CH, CH),
            preferred_element_type=F32,
        )
    out_ref[0] = total.astype(BF16).reshape(NCH, OUTW, CH)

    @pl.when(guest)
    def _():
        for c in range(NCH):
            swap(lt, xl, SW_L, c).wait_send()
            swap(rt, xr, SW_R, c).wait_send()
            map_home(c).wait_send()
        partial_home(LAST).wait_send()

    for c in range(NCH):
        across(xl, X_L, c).wait_send()
        across(xr, X_R, c).wait_send()
        for kv, z_sem, c_sem, f_sem in ((kvs, KS_Z, KS_C, KS_F), (kvc, KC_Z, KC_C, KC_F)):
            to_z(kv, z_sem, c).wait_send()
            to_sibling(kv, c_sem, c).wait_send()
            onward(kv, f_sem, c).wait_send()
        mixed_across(c).wait_send()
        if c != LAST:
            partial_across(c).wait_send()
    so_copy.wait_send()
    ra_copy.wait_send()

    @pl.when(home)
    def _():
        partial_across(LAST).wait_send()

    @pl.when(band > 0)
    def _():
        map_above().wait_send()

    @pl.when(band < 3)
    def _():
        map_below().wait_send()


def fused_body(*arrays):
    hbm = pl.BlockSpec(memory_space=pl.ANY)
    return pl.pallas_call(
        fused_kernel,
        out_shape=jax.ShapeDtypeStruct((1, NCH, OUTW, CH), BF16),
        in_specs=[hbm] * len(arrays),
        out_specs=pl.BlockSpec(memory_space=pltpu.VMEM),
        scratch_shapes=[
            pltpu.VMEM((2, ROWS, FEAT), BF16),
            pltpu.VMEM((2, ROWS, FEAT), BF16),
            pltpu.VMEM((3, DIM, COLS), BF16),
            pltpu.VMEM((3, DIM, COLS), BF16),
            pltpu.VMEM((2, COLS, DIM), BF16),
            pltpu.VMEM((COLS, DIM), BF16),
            pltpu.VMEM((2, FEAT, CH), BF16),
            pltpu.VMEM((3, 3, CH, CH), BF16),
            pltpu.VMEM((NCH, 2, 128, 256), BF16),
            pltpu.VMEM((4, NCH, 4, 128, 128), BF16),
            pltpu.VMEM((4, NCH, 4, 128, 128), BF16),
            pltpu.VMEM((2 * NCH, 1, 256), F32),
            pltpu.VMEM((2 * NCH, 1, 256), F32),
            pltpu.VMEM((2 * NCH, 128, 128), F32),
            pltpu.VMEM((2, ROWS, COLS), BF16),
            pltpu.VMEM((ROWS, DIM), BF16),
            pltpu.VMEM((COLS, CH), BF16),
            pltpu.VMEM((NCH, CHUNK, CH), F32),
            pltpu.VMEM((NCH, WIN, CH), F32),
            pltpu.VMEM((NCH, WIN, CH), BF16),
            pltpu.VMEM((NCH, WIN, CH), BF16),
            pltpu.VMEM((NCH, WIN, CH), BF16),
            pltpu.VMEM((NCH + 2, 96, CH), BF16),
            pltpu.VMEM((NCH + 2, 96, CH), F32),
            pltpu.SemaphoreType.DMA((N_SEMS,)),
            pltpu.SemaphoreType.DMA((N_SEMS,)),
            pltpu.SemaphoreType.DMA((N_LOCAL,)),
        ],
        compiler_params=pltpu.CompilerParams(
            collective_id=0, has_side_effects=True, vmem_limit_bytes=56 * 2**20
        ),
        cost_estimate=pl.CostEstimate(
            flops=3 * 10**9, bytes_accessed=6 * 10**6, transcendentals=5 * 10**6
        ),
        name="decoder",
    )(*arrays)


def layer_norm(values):
    widened = values.astype(F32)
    centred = widened - jnp.mean(widened, axis=-1, keepdims=True)
    variance = jnp.mean(centred * centred, axis=-1, keepdims=True)
    return (centred * lax.rsqrt(variance + 1e-06)).astype(BF16)


def project_rows(normed, weight):
    return jnp.dot(normed, weight, preferred_element_type=F32).astype(BF16)


def attend_keys(running, queries, keys_rows, values_rows):
    maxima, totals, accumulated = running
    query_count = queries.shape[0]
    head_count = queries.shape[1] // HD
    key_count = keys_rows.shape[0]
    scores = jnp.einsum(
        "qhd,khd->hqk",
        queries.reshape(query_count, head_count, HD),
        keys_rows.reshape(key_count, head_count, HD),
        preferred_element_type=F32,
    ) * HD ** (-0.5)
    new_maxima = jnp.maximum(maxima, jnp.max(scores, axis=2))
    correction = jnp.exp(maxima - new_maxima)
    expanded = jnp.exp(scores - new_maxima[:, :, None])
    totals = totals * correction + jnp.sum(expanded, axis=2)
    mixed = jnp.einsum(
        "hqk,khd->qhd",
        expanded.astype(BF16),
        values_rows.reshape(key_count, head_count, HD),
        preferred_element_type=F32,
    )
    accumulated = (
        accumulated.reshape(query_count, head_count, HD) * correction.T[:, :, None] + mixed
    )
    return (new_maxima, totals, accumulated.reshape(query_count, head_count * HD))


def attention_over(queries, pieces):
    query_count = queries.shape[0]
    head_count = queries.shape[1] // HD
    running = (
        jnp.full((head_count, query_count), -jnp.inf, F32),
        jnp.zeros((head_count, query_count), F32),
        jnp.zeros(queries.shape, F32),
    )
    for piece in pieces:
        running = attend_keys(running, queries, piece[0], piece[1])
    maxima, totals, accumulated = running
    normalized_rows = accumulated.reshape(query_count, head_count, HD) / totals.T[:, :, None]
    return normalized_rows.reshape(query_count, head_count * HD).astype(BF16)


def shifted_pieces(value, axis):
    count = lax.axis_size(axis)
    return [value] + [
        lax.ppermute(value, axis, [(i, (i + shift) % count) for i in range(count)])
        for shift in range(1, count)
    ]


def gather_columns(value, axis):
    count = lax.axis_size(axis)
    index = lax.axis_index(axis)
    width = value.shape[-1]
    whole = jnp.zeros(value.shape[:-1] + (count * width,), value.dtype)
    for shift, piece in enumerate(shifted_pieces(value, axis)):
        start = lax.rem(index - shift + count, count) * width
        whole = lax.dynamic_update_slice_in_dim(whole, piece, start, axis=value.ndim - 1)
    return whole


def sum_over(value, axis):
    total = value.astype(F32)
    for piece in shifted_pieces(value, axis)[1:]:
        total = total + piece.astype(F32)
    return total


def with_border_rows(cells):
    count = lax.axis_size("blk")
    up = [(i, i + 1) for i in range(count - 1)]
    down = [(i + 1, i) for i in range(count - 1)]
    return jnp.concatenate(
        [lax.ppermute(cells[-1:], "blk", up), cells, lax.ppermute(cells[:1], "blk", down)], axis=0
    )


def general_body(
    left_tokens, right_tokens, self_qkv, self_out, cross_qkv, cross_out, reassemble, conv_weight
):
    tiles = lax.axis_size("tile")
    tile_index = lax.axis_index("tile")
    token_count = left_tokens.shape[1]
    left_full = gather_columns(left_tokens[0], "tile")
    right_full = gather_columns(right_tokens[0], "tile")
    reassemble_full = gather_columns(reassemble.T, "tile").T
    left_normed = layer_norm(left_full)
    right_normed = layer_norm(right_full)
    self_query = project_rows(left_normed, self_qkv[0])
    self_pieces = shifted_pieces(
        jnp.stack([project_rows(left_normed, self_qkv[1]), project_rows(left_normed, self_qkv[2])]),
        "blk",
    )
    cross_pieces = shifted_pieces(
        jnp.stack(
            [project_rows(right_normed, cross_qkv[1]), project_rows(right_normed, cross_qkv[2])]
        ),
        "blk",
    )
    self_mixed = attention_over(self_query, self_pieces)
    self_term = jnp.dot(self_mixed, self_out, preferred_element_type=F32)
    self_sum = sum_over(self_term.astype(BF16), "tile")
    updated = (left_full.astype(F32) + self_sum).astype(BF16)
    cross_query = project_rows(layer_norm(updated), cross_qkv[0])
    cross_mixed = attention_over(cross_query, cross_pieces)
    cross_term = jnp.dot(cross_mixed, cross_out, preferred_element_type=F32)
    cross_sum = sum_over(cross_term.astype(BF16), "tile")
    final_tokens = (updated.astype(F32) + cross_sum).astype(BF16)
    band_rows = token_count // GRID_W
    column_count = GRID_W // tiles
    grid = jnp.pad(final_tokens.reshape(band_rows, GRID_W, -1), ((0, 0), (1, 1), (0, 0)))
    window = lax.dynamic_slice_in_dim(grid, tile_index * column_count, column_count + 2, axis=1)
    wide_map = jnp.dot(
        window.reshape(band_rows * (column_count + 2), -1),
        reassemble_full,
        preferred_element_type=F32,
    )
    wide_map = wide_map.astype(BF16).reshape(band_rows, column_count + 2, CH)
    feature_map = wide_map[:, 1 : column_count + 1]
    padded = with_border_rows(jnp.maximum(wide_map, jnp.zeros((), BF16)))
    stacked = jnp.concatenate(
        [
            padded[row_shift : row_shift + band_rows, col_shift : col_shift + column_count]
            for row_shift in range(3)
            for col_shift in range(3)
        ],
        axis=-1,
    )
    convolved = jnp.dot(
        stacked.reshape(band_rows * column_count, 9 * CH),
        conv_weight.reshape(9 * CH, CH),
        preferred_element_type=F32,
    )
    joined = feature_map.astype(F32) + convolved.reshape(band_rows, column_count, CH)
    return joined.astype(BF16)[None]


def whole_program(mesh, *arrays):
    shape = mesh.shape
    left, qkv = arrays[0], arrays[2]
    fits = (
        shape["blk"] == 4
        and shape["tile"] == 2
        and shape["pair"] == 2
        and left.shape[0] == 2 * shape["groups"]
        and left.shape[1] == 4 * ROWS
        and left.shape[2] == DIM
        and qkv.shape[2] == 2 * COLS
    )
    placed = (
        P(("groups", "pair"), "blk", "tile"),
        P(("groups", "pair"), "blk", "tile"),
        P(None, None, "tile"),
        P("tile", None),
        P(None, None, "tile"),
        P("tile", None),
        P("tile", None),
        P(),
    )
    return jax.shard_map(
        fused_body if fits else general_body,
        mesh=mesh,
        in_specs=placed,
        out_specs=P(("groups", "pair"), "blk", "tile", None),
        check_vma=False,
    )(*arrays)


def solution(mesh):
    return functools.partial(whole_program, mesh)
```
